512 devices in a mesh: gx: 8 (over z_hi, y), gy: 4 (over x), gz: 16 (over z_lo, core).
Axes of the slice: x: 4, y: 4, z: 16 (z_hi: 2, z_lo: 8; z = z_hi * 8 + z_lo), core: 2. Of those that a mesh axis runs over, the one named last changes fastest.
Arguments:
- right_side: float32 [64, 32, 16, 4096], P(None, 'gx', 'gy', 'gz'), may hold values from -6 to 6
- stiffness: float32 [32, 16, 4096], P('gx', 'gy', 'gz'), may hold values from 0.35 to 2.5
- reaction: float32 [32, 16, 4096], P('gx', 'gy', 'gz'), may hold values from 0.1 to 1
- deflation: bfloat16 [128, 32, 16, 4096], P(None, 'gx', 'gy', 'gz'), may hold values from -0.09375 to 0.09375
- coarse_blocks: bfloat16 [512, 7, 128, 128], P(('gx', 'gy', 'gz')), may hold values from -3 to 4, as said below
- row_owner: int32 [512], P(('gx', 'gy', 'gz')), may hold values from 0 to 15, as said below
- neighbours: int32 [512, 6], P(('gx', 'gy', 'gz')), may hold values from 0 to 15, as said below
Outputs:
- solution: float32 [64, 32, 16, 4096], P(None, 'gx', 'gy', 'gz')
- residual: float32 [64, 32, 16, 4096], P(None, 'gx', 'gy', 'gz')
The draws below stay inside these ranges and needn't reach their ends.
Inputs may be any that keep to these rules, and one draw needn't show every extreme that they name: `row_owner`: each entry is a multiple of 3. For the block row at position c of its line, entries 0 and 1 are (c - 1) and (c + 1) modulo 16, its neighbours along the third dimension; entries 2 to 5 are any positions in the line. `coarse_blocks`: blocks of order one; the diagonal block is near 2 times the identity.
All inputs are finite; a program needn't handle non-finite values.
Results may differ from the reference program's by a relative error of at most 0.013.
Values may be sent and summed in bfloat16 or wider, within the bound.
A program may use at most 64 MiB of HBM per device.

```python
import math
import jax
import jax.numpy as jnp

R = 64
K = 128
CX = 4
CY = 4
CZ = 256
ITERS = 2
SWEEPS = 2
CHEB = 2
NSUB = 512
LINE = 16
NX = 32
NY = 16
NZ = 4096
N_GX = 8
N_GY = 4
N_GZ = 16


def draw_row_owner(key, part):
    labels = 3 * jax.random.randint(key, (NSUB,), 0, (LINE + 2) // 3)
    labels = labels.at[0].set(3 * ((LINE - 1) // 3))
    return labels.astype(jnp.int32)


def draw_neighbours(key, part):
    places = (jnp.arange(NSUB) % LINE).astype(jnp.int32)
    lower = ((places + LINE - 1) % LINE).astype(jnp.int32)
    upper = ((places + 1) % LINE).astype(jnp.int32)
    others = jax.random.randint(key, (NSUB, 4), 0, LINE).astype(jnp.int32)
    others = others.at[0, 0].set(0)
    others = others.at[0, 1].set(LINE - 1)
    return jnp.concatenate([lower[:, None], upper[:, None], others], axis=1).astype(jnp.int32)


def draw_coarse_blocks(key, part):
    entries = 0.4 * jax.random.normal(key, (NSUB, 7, K, K), jnp.float32) / math.sqrt(K)
    identity = jnp.eye(K, dtype=jnp.float32)
    entries = entries.at[:, 0].add(2.0 * identity)
    return entries.astype(jnp.bfloat16)


def outer_slices():
    places = jnp.arange(NZ) % CZ
    return (places == 0) | (places == CZ - 1)


def draw_right_side(key, part):
    facing = outer_slices()[None, None, None, :]
    factor = jnp.where(facing, 2.5, 0.1).astype(jnp.float32)
    values = factor * jax.random.normal(key, (R, NX, NY, NZ), jnp.float32)
    return jnp.clip(values, -6.0, 6.0).astype(jnp.float32)


def draw_stiffness(key, part):
    facing = outer_slices()[None, None, :]
    bottom = jnp.where(facing, 1.0, 0.35).astype(jnp.float32)
    summit = jnp.where(facing, 2.5, 0.7).astype(jnp.float32)
    fraction = jax.random.uniform(key, (NX, NY, NZ), jnp.float32, 0.0, 1.0)
    values = jnp.exp(jnp.log(bottom) + fraction * (jnp.log(summit) - jnp.log(bottom)))
    return jnp.clip(values, 0.35, 2.5).astype(jnp.float32)


def block_scale(own_key, shape, split, low, top_value):
    def one(axis_at, parts):
        heights = jax.random.uniform(jax.random.fold_in(jax.random.fold_in(own_key, 6), axis_at), (parts,), jnp.float32, low / len(split), top_value / len(split))
        return jnp.repeat(jnp.exp(heights), shape[axis_at] // parts).reshape((-1,) + (1,) * (len(shape) - axis_at - 1))

    gain = one(*split[0])
    for cut in split[1:]:
        gain = gain * one(*cut)
    return gain


def scatter_about(rng, shape, deviation, reach, split=(), kind=jnp.bfloat16):
    array = deviation * jax.random.normal(rng, shape, jnp.float32)
    if split:
        array = array * block_scale(rng, shape, split, -0.22, 0.18)
    return jnp.clip(array, -reach, reach).astype(kind)


def setup_inputs(seed: int = 0) -> dict:
    splits = jax.random.split(jax.random.key(seed), 8)
    right_side = draw_right_side(jax.random.fold_in(splits[7], 71), 0)
    stiffness = draw_stiffness(jax.random.fold_in(splits[7], 71), 0)
    reaction = jnp.clip(jnp.exp(math.log(1.0) - 2.3025851 * jax.random.uniform(splits[2], (NX, NY, NZ), jnp.float32) ** block_scale(splits[2], (NX, NY, NZ), ((0, 8), (1, 4), (2, 16)), -0.2, 0.2)), 0.1, 1.0)
    deflation = scatter_about(splits[3], (K, NX, NY, NZ), (CX * CY * CZ) ** -0.5, 0.09375, ((1, 8), (2, 4), (3, 16)))
    coarse_blocks = draw_coarse_blocks(jax.random.fold_in(splits[7], 71), 0)
    row_owner = draw_row_owner(jax.random.fold_in(splits[7], 71), 0)
    neighbours = draw_neighbours(jax.random.fold_in(splits[7], 71), 0)
    return {"right_side": right_side, "stiffness": stiffness, "reaction": reaction, "deflation": deflation, "coarse_blocks": coarse_blocks, "row_owner": row_owner, "neighbours": neighbours}


RELAX_WEIGHT = 0.8
CENTRE_VALUE = 2.0
HALF_WIDTH = 1.0


def stencil_sum(padded):
    return (padded[:, 2:, 1:-1, 1:-1] + padded[:, :-2, 1:-1, 1:-1]
            + padded[:, 1:-1, 2:, 1:-1] + padded[:, 1:-1, :-2, 1:-1]
            + padded[:, 1:-1, 1:-1, 2:] + padded[:, 1:-1, 1:-1, :-2])


def apply_global(values, stiffness, reaction):
    scaled = stiffness * values
    padded = jnp.pad(scaled, ((0, 0), (1, 1), (1, 1), (1, 1)))
    return stiffness * (6.0 * scaled - stencil_sum(padded)) + reaction * values


def apply_blocked(values, stiffness, reaction):
    scaled = stiffness * values
    beside = jnp.zeros_like(scaled)
    for dimension, extent in ((1, CX), (2, CY), (3, CZ)):
        length = scaled.shape[dimension]
        places = jnp.arange(length)
        layout = [1, 1, 1, 1]
        layout[dimension] = length
        upper_keep = (places % extent != extent - 1).astype(scaled.dtype).reshape(layout)
        lower_keep = (places % extent != 0).astype(scaled.dtype).reshape(layout)
        beside = beside + jnp.roll(scaled, -1, dimension) * upper_keep + jnp.roll(scaled, 1, dimension) * lower_keep
    return stiffness * (6.0 * scaled - beside) + reaction * values


def to_subdomains(values):
    leading = values.shape[0]
    blocked = values.reshape(leading, N_GX, CX, N_GY, CY, N_GZ, CZ)
    return blocked.transpose(1, 3, 5, 0, 2, 4, 6).reshape(NSUB, leading, CX * CY * CZ)


def from_subdomains(values):
    leading = values.shape[1]
    blocked = values.reshape(N_GX, N_GY, N_GZ, leading, CX, CY, CZ)
    return blocked.transpose(3, 0, 4, 1, 5, 2, 6).reshape(leading, NX, NY, NZ)


def coarse_apply(values, blocks_full, row_owner, neighbours):
    line_count = NSUB // LINE
    values_full = values.astype(jnp.float32).reshape(line_count, LINE, R, K)
    owners = row_owner.reshape(line_count, LINE)
    near = neighbours.reshape(line_count, LINE, 6)
    places = jnp.arange(LINE).astype(jnp.int32)
    chosen = (near[:, :, :, None] == places[None, None, None, :]) & (owners[:, :, None, None] == owners[:, None, None, :])
    picked = jnp.einsum("lpjq,lqrk->lpjrk", chosen.astype(jnp.float32), values_full)
    blocks = blocks_full.reshape(line_count, LINE, 7, K, K)
    result = jnp.einsum("lprk,lpkm->lprm", values_full, blocks[:, :, 0]) + jnp.einsum("lpjrk,lpjkm->lprm", picked, blocks[:, :, 1:])
    return result.reshape(NSUB, R, K)


def chebyshev(coarse_rhs, apply_coarse):
    target = coarse_rhs.astype(jnp.float32)
    ratio_now = HALF_WIDTH / CENTRE_VALUE
    direction = target / CENTRE_VALUE
    coarse = direction
    for step_index in range(CHEB):
        ratio_next = 1.0 / (2.0 * CENTRE_VALUE / HALF_WIDTH - ratio_now)
        misfit = target - apply_coarse(coarse.astype(jnp.bfloat16))
        direction = ratio_next * ratio_now * direction + (2.0 * ratio_next / HALF_WIDTH) * misfit
        coarse = coarse + direction
        ratio_now = ratio_next
    return coarse.astype(jnp.bfloat16)


def reference(right_side, stiffness, reaction, deflation, coarse_blocks, row_owner, neighbours):
    diagonal = 6.0 * stiffness * stiffness + reaction
    vectors = to_subdomains(deflation).astype(jnp.float32)
    blocks_full = coarse_blocks.astype(jnp.float32)

    def apply_coarse(values):
        return coarse_apply(values, blocks_full, row_owner, neighbours)

    solution = jnp.zeros(right_side.shape, jnp.float32)
    residual = right_side
    for iteration in range(ITERS):
        smooth = RELAX_WEIGHT * residual / diagonal
        for sweep_index in range(SWEEPS - 1):
            smooth = smooth + RELAX_WEIGHT * (residual - apply_blocked(smooth, stiffness, reaction)) / diagonal
        rounded = to_subdomains(residual.astype(jnp.bfloat16)).astype(jnp.float32)
        coarse_rhs = jnp.einsum("src,skc->srk", rounded, vectors).astype(jnp.bfloat16)
        coarse = chebyshev(coarse_rhs, apply_coarse)
        prolong = from_subdomains(jnp.einsum("srk,skc->src", coarse.astype(jnp.float32), vectors))
        update = smooth + prolong
        solution = solution + update
        residual = residual - apply_global(update, stiffness, reaction)
    return solution, residual
```

```python
import functools

import jax
import jax.numpy as jnp
from jax import lax
from jax.experimental import pallas as pl
from jax.experimental.pallas import tpu as pltpu
from jax.sharding import PartitionSpec as P

ITERS = 2
CHEB = 2

RELAX_WEIGHT = 0.8
CENTRE_VALUE = 2.0
HALF_WIDTH = 1.0

MESH = pl.DeviceIdType.MESH
F32 = jnp.float32
BF16 = jnp.bfloat16


def flip(place, bits):
    bit = 1
    while bit <= bits:
        if bits & bit:
            place = place + bit - 2 * bit * ((place // bit) % 2)
        bit *= 2
    return place


def kernel(
    sizes,
    r_ref,
    s_ref,
    react_ref,
    z_ref,
    b_ref,
    owner_ref,
    near_ref,
    sol_ref,
    res_ref,
    coef,
    wpad,
    smooth,
    blocks,
    owners,
    line0,
    line1,
    line2,
    line3,
    xsend,
    xrecv,
    ysend,
    yrecv,
    zsend,
    zrecv,
    owner_send_sem,
    owner_recv_sem,
    line_send_sem,
    line_recv_sem,
    face_send_sem,
    face_recv_sem,
):
    n_gx, n_gy, n_gz, cx, cy, cz = sizes
    rows = r_ref.shape[0]
    n_chips = n_gz // 2
    pad_y = cy + 2
    a, b, g = lax.axis_index("gx"), lax.axis_index("gy"), lax.axis_index("gz")
    chip, core = g // 2, g % 2
    partner = chip * 2 + 1 - core
    line = (line0, line1, line2, line3)

    def at_line(place):
        return {"gz": place}

    barrier = pltpu.get_barrier_semaphore()
    for step in range(1, n_gz):
        pl.semaphore_signal(
            barrier, inc=1, device_id=at_line((g + step) % n_gz), device_id_type=MESH
        )
    places = (("gx", a, n_gx), ("gy", b, n_gy))
    for name, place, count in places:

        @pl.when(place > 0)
        def _():
            pl.semaphore_signal(
                barrier, inc=1, device_id={name: place - 1}, device_id_type=MESH
            )

        @pl.when(place < count - 1)
        def _():
            pl.semaphore_signal(
                barrier, inc=1, device_id={name: place + 1}, device_id_type=MESH
            )

    stiff = s_ref[...]
    diagonal = 6.0 * stiff * stiff + react_ref[...]
    relax = RELAX_WEIGHT / diagonal
    coef[0] = stiff
    coef[1] = diagonal
    coef[2] = (2.0 - RELAX_WEIGHT) * relax
    coef[3] = stiff * relax

    lane = lax.broadcasted_iota(jnp.int32, (rows, cz), 1)
    narrow = lax.broadcasted_iota(jnp.int32, (rows, 128), 1)

    def cols(j):
        return pl.ds(pl.multiple_of(j * cz, cz), cz)

    def padded(j):
        x, y = j // cy, j % cy
        return ((x + 1) * pad_y + y + 1) * cz

    def pcols(offset):
        return pl.ds(pl.multiple_of(offset, cz), cz)

    def row(which, j):
        return coef[which, pl.ds(j, 1), :]

    def beside(offset):
        centre = wpad[:, pcols(offset)]
        total = wpad[:, pcols(offset + pad_y * cz)] + wpad[:, pcols(offset - pad_y * cz)]
        total = total + wpad[:, pcols(offset + cz)] + wpad[:, pcols(offset - cz)]
        total = total + jnp.where(lane == cz - 1, 0.0, pltpu.roll(centre, cz - 1, 1))
        return total + jnp.where(lane == 0, 0.0, pltpu.roll(centre, 1, 1))

    def each(first, count, body):
        def step(i, carry):
            body(first + i)
            return carry

        lax.fori_loop(0, count, step, 0)

    zero_row = jnp.zeros((rows, pad_y * cz), F32)
    wpad[:, pl.ds(0, pad_y * cz)] = zero_row
    wpad[:, pl.ds((cx + 1) * pad_y * cz, pad_y * cz)] = zero_row
    for x in range(cx):
        wpad[:, pl.ds((x + 1) * pad_y * cz, cz)] = jnp.zeros((rows, cz), F32)
        wpad[:, pl.ds(((x + 2) * pad_y - 1) * cz, cz)] = jnp.zeros((rows, cz), F32)

    faces = (("gx", a, n_gx, xrecv), ("gy", b, n_gy, yrecv), ("gz", g, n_gz, zrecv))
    for it in range(ITERS):
        for name, place, count, recv in faces:

            @pl.when(place == 0)
            def _():
                recv[it, 0] = jnp.zeros(recv.shape[2:], recv.dtype)

            @pl.when(place == count - 1)
            def _():
                recv[it, 1] = jnp.zeros(recv.shape[2:], recv.dtype)

    def restrict(field):
        width = cy * cz
        total = jnp.zeros((rows, z_ref.shape[0]), F32)
        for x in range(cx):
            part = pl.ds(x * width, width)
            total = total + lax.dot_general(
                field[:, part].astype(BF16),
                z_ref[:, part],
                (((1,), (1,)), ((), ())),
                preferred_element_type=F32,
            )
        return total.astype(BF16)

    def line_copy(turn, slot, sem, target):
        return pltpu.make_async_remote_copy(
            src_ref=line[turn].at[slot],
            dst_ref=line[turn].at[slot],
            send_sem=line_send_sem.at[turn, sem],
            recv_sem=line_recv_sem.at[turn, slot],
            device_id=at_line(target),
            device_id_type=MESH,
        )

    def line_start(turn, value):
        line[turn][g] = value
        for bits in range(n_chips - 1, 0, -1):
            line_copy(turn, g, bits, flip(chip, bits) * 2 + core).start()
        line_copy(turn, g, 0, partner).start()

    def line_finish(turn):
        for bits in range(1, n_chips):
            source = flip(chip, bits) * 2 + core
            line_copy(turn, source, 0, partner).wait_recv()
            line_copy(turn, source, n_chips + bits, partner).start()
        line_copy(turn, partner, 0, partner).wait_recv()
        for bits in range(1, n_chips):
            source = flip(chip, bits) * 2 + 1 - core
            line_copy(turn, source, 0, partner).wait_recv()

    def line_drain(turn):
        for sem in range(n_chips):
            line_copy(turn, g, sem, partner).wait_send()
        for bits in range(1, n_chips):
            line_copy(turn, g, n_chips + bits, partner).wait_send()

    def face_copy(it, axis, side, send, recv, name, target):
        return pltpu.make_async_remote_copy(
            src_ref=send.at[it, side],
            dst_ref=recv.at[it, 1 - side],
            send_sem=face_send_sem.at[it, axis, side],
            recv_sem=face_recv_sem.at[it, axis, 1 - side],
            device_id={name: target},
            device_id_type=MESH,
        )

    exchange = (
        (0, "gx", a, n_gx, xsend, xrecv),
        (1, "gy", b, n_gy, ysend, yrecv),
        (2, "gz", g, n_gz, zsend, zrecv),
    )

    def face_start(it, which):
        axis, name, place, count, send, recv = exchange[which]

        @pl.when(place > 0)
        def _():
            face_copy(it, axis, 0, send, recv, name, place - 1).start()

        @pl.when(place < count - 1)
        def _():
            face_copy(it, axis, 1, send, recv, name, place + 1).start()

    def face_wait(it, which):
        axis, name, place, count, send, recv = exchange[which]

        @pl.when(place > 0)
        def _():
            face_copy(it, axis, 1, send, recv, name, place - 1).wait_recv()

        @pl.when(place < count - 1)
        def _():
            face_copy(it, axis, 0, send, recv, name, place + 1).wait_recv()

    def face_drain(it, which):
        axis, name, place, count, send, recv = exchange[which]

        @pl.when(place > 0)
        def _():
            face_copy(it, axis, 0, send, recv, name, place - 1).wait_send()

        @pl.when(place < count - 1)
        def _():
            face_copy(it, axis, 1, send, recv, name, place + 1).wait_send()

    def relaxed(field):
        def scale(j):
            wpad[:, pcols(padded(j))] = row(3, j) * field[:, cols(j)]

        def combine(j):
            smooth[:, cols(j)] = row(2, j) * field[:, cols(j)] + row(3, j) * beside(padded(j))

        each(0, cx * cy, scale)
        each(0, cx * cy, combine)

    def apply_coarse(turn, value):
        picked = [value] + [line[turn][near_ref[0, k]] for k in range(6)]
        return jnp.dot(
            jnp.concatenate(picked, axis=1), blocks[...], preferred_element_type=F32
        )

    def owner_copy(target):
        return pltpu.make_async_remote_copy(
            src_ref=owners.at[g],
            dst_ref=owners.at[g],
            send_sem=owner_send_sem,
            recv_sem=owner_recv_sem,
            device_id=at_line(target),
            device_id_type=MESH,
        )

    owners[g] = jnp.full((1, 128), owner_ref[0], jnp.int32)
    for it in range(ITERS):
        field = r_ref if it == 0 else res_ref
        coarse_rhs = restrict(field)
        if it == 0:
            peers = n_gz - 1
            for name, place, count in places:
                for way in (place, count - 1 - place):
                    peers = peers + (way + count - 1) // count
            pl.semaphore_wait(barrier, peers)
            for step in range(1, n_gz):
                owner_copy((g + step) % n_gz).start()
        line_start(CHEB * it, coarse_rhs)
        relaxed(field)
        if it == 0:
            others = owners.at[pl.ds(0, n_gz - 1)]
            pltpu.make_async_copy(others, others, owner_recv_sem).wait()
            blocks[pl.ds(0, 128), :] = b_ref[pl.ds(0, 128), :]
            for k in range(6):
                keep = owners[near_ref[0, k]] == owner_ref[0]
                part = pl.ds((k + 1) * 128, 128)
                blocks[part, :] = jnp.where(keep, b_ref[part, :].astype(F32), 0.0).astype(BF16)

        target = coarse_rhs.astype(F32)
        ratio_now = HALF_WIDTH / CENTRE_VALUE
        direction = target / CENTRE_VALUE
        coarse = direction
        for step in range(CHEB):
            ratio_next = 1.0 / (2.0 * CENTRE_VALUE / HALF_WIDTH - ratio_now)
            turn = CHEB * it + step
            line_finish(turn)
            if step == 0:
                misfit = target - apply_coarse(turn, coarse_rhs) / CENTRE_VALUE
            else:
                misfit = target - apply_coarse(turn, coarse.astype(BF16))
            direction = (
                ratio_next * ratio_now * direction + 2.0 * ratio_next / HALF_WIDTH * misfit
            )
            coarse = coarse + direction
            ratio_now = ratio_next
            if step < CHEB - 1:
                line_start(turn + 1, coarse.astype(BF16))
        coarse = coarse.astype(BF16)

        def correct(j):
            update = smooth[:, cols(j)] + jnp.dot(
                coarse, z_ref[:, cols(j)], preferred_element_type=F32
            )
            smooth[:, cols(j)] = update
            wpad[:, pcols(padded(j))] = row(0, j) * update
            if it == 0:
                sol_ref[:, cols(j)] = update
            else:
                sol_ref[:, cols(j)] = sol_ref[:, cols(j)] + update

        each(0, cy, correct)
        each((cx - 1) * cy, cy, correct)
        for side, x in enumerate((0, cx - 1)):
            xsend[it, side] = wpad[:, pl.ds(((x + 1) * pad_y + 1) * cz, cy * cz)].astype(BF16)
        face_start(it, 0)
        each(cy, (cx - 2) * cy, correct)
        for side, y in enumerate((0, cy - 1)):
            for x in range(cx):
                ysend[it, side, :, pl.ds(x * cz, cz)] = wpad[
                    :, pl.ds(((x + 1) * pad_y + y + 1) * cz, cz)
                ].astype(BF16)
        face_start(it, 1)

        def gather(j, carry):
            low, high = carry
            first = wpad[:, pl.ds(pl.multiple_of(padded(j), 128), 128)]
            last = wpad[:, pl.ds(pl.multiple_of(padded(j) + cz - 128, 128), 128)]
            low = jnp.where(narrow == j, pltpu.roll(first, j, 1), low)
            high = jnp.where(narrow == j, pltpu.roll(last, j + 1, 1), high)
            return low, high

        empty = jnp.zeros((rows, 128), F32)
        low, high = lax.fori_loop(0, cx * cy, gather, (empty, empty))
        zsend[it, 0] = low.astype(BF16)
        zsend[it, 1] = high.astype(BF16)
        face_start(it, 2)

        def apply_inside(j):
            res_ref[:, cols(j)] = (
                field[:, cols(j)]
                - row(1, j) * smooth[:, cols(j)]
                + row(0, j) * beside(padded(j))
            )

        each(0, cx * cy, apply_inside)

        face_wait(it, 2)
        zlow, zhigh = zrecv[it, 0].astype(F32), zrecv[it, 1].astype(F32)

        def add_z(j):
            first = pl.ds(pl.multiple_of(j * cz, 128), 128)
            last = pl.ds(pl.multiple_of(j * cz + cz - 128, 128), 128)
            scale = coef[0, pl.ds(j, 1), :]
            res_ref[:, first] = res_ref[:, first] + jnp.where(
                narrow == 0, scale[:, :128] * pltpu.roll(zlow, (128 - j) % 128, 1), 0.0
            )
            res_ref[:, last] = res_ref[:, last] + jnp.where(
                narrow == 127, scale[:, cz - 128 :] * pltpu.roll(zhigh, 127 - j, 1), 0.0
            )

        each(0, cx * cy, add_z)
        face_wait(it, 1)
        for side, y in enumerate((0, cy - 1)):
            for x in range(cx):
                j = x * cy + y
                part = pl.ds(j * cz, cz)
                res_ref[:, part] = res_ref[:, part] + coef[0, pl.ds(j, 1), :] * yrecv[
                    it, side, :, pl.ds(x * cz, cz)
                ].astype(F32)
        face_wait(it, 0)
        for side, x in enumerate((0, cx - 1)):
            for y in range(cy):
                j = x * cy + y
                part = pl.ds(j * cz, cz)
                res_ref[:, part] = res_ref[:, part] + coef[0, pl.ds(j, 1), :] * xrecv[
                    it, side, :, pl.ds(y * cz, cz)
                ].astype(F32)

    for it in range(ITERS):
        for step in range(CHEB):
            line_drain(CHEB * it + step)
        for which in range(3):
            face_drain(it, which)
    others = owners.at[pl.ds(0, n_gz - 1)]
    pltpu.make_async_copy(others, others, owner_send_sem).wait()


def local(sizes, right_side, stiffness, reaction, deflation, coarse_blocks, row_owner, neighbours):
    n_gx, n_gy, n_gz = sizes
    rows, cx, cy, cz = right_side.shape
    cells = cx * cy * cz
    vectors = deflation.shape[0]
    vmem = pl.BlockSpec(memory_space=pltpu.VMEM)
    smem = pl.BlockSpec(memory_space=pltpu.SMEM)
    turns = ITERS * CHEB
    solution, residual = pl.pallas_call(
        functools.partial(kernel, (n_gx, n_gy, n_gz, cx, cy, cz)),
        out_shape=(jax.ShapeDtypeStruct((rows, cells), F32),) * 2,
        in_specs=[vmem] * 5 + [smem] * 2,
        out_specs=(vmem, vmem),
        scratch_shapes=[
            pltpu.VMEM((4, cx * cy, cz), F32),
            pltpu.VMEM((rows, (cx + 2) * (cy + 2) * cz), F32),
            pltpu.VMEM((rows, cells), F32),
            pltpu.VMEM((7 * vectors, vectors), BF16),
            pltpu.VMEM((n_gz, 1, 128), jnp.int32),
            *[pltpu.VMEM((n_gz, rows, vectors), BF16)] * turns,
            pltpu.VMEM((ITERS, 2, rows, cy * cz), BF16),
            pltpu.VMEM((ITERS, 2, rows, cy * cz), BF16),
            pltpu.VMEM((ITERS, 2, rows, cx * cz), BF16),
            pltpu.VMEM((ITERS, 2, rows, cx * cz), BF16),
            pltpu.VMEM((ITERS, 2, rows, 128), BF16),
            pltpu.VMEM((ITERS, 2, rows, 128), BF16),
            pltpu.SemaphoreType.DMA,
            pltpu.SemaphoreType.DMA,
            pltpu.SemaphoreType.DMA((turns, n_gz)),
            pltpu.SemaphoreType.DMA((turns, n_gz)),
            pltpu.SemaphoreType.DMA((ITERS, 3, 2)),
            pltpu.SemaphoreType.DMA((ITERS, 3, 2)),
        ],
        compiler_params=pltpu.CompilerParams(
            collective_id=0, has_side_effects=True, vmem_limit_bytes=40 * 1024 * 1024
        ),
        name="schwarz",
    )(
        right_side.reshape(rows, cells),
        stiffness.reshape(cx * cy, cz),
        reaction.reshape(cx * cy, cz),
        deflation.reshape(vectors, cells),
        coarse_blocks.reshape(7 * vectors, vectors),
        row_owner,
        neighbours,
    )
    return solution.reshape(right_side.shape), residual.reshape(right_side.shape)


def solution(mesh):
    sizes = tuple(mesh.shape[name] for name in ("gx", "gy", "gz"))
    return jax.shard_map(
        functools.partial(local, sizes),
        mesh=mesh,
        in_specs=(
            P(None, "gx", "gy", "gz"),
            P("gx", "gy", "gz"),
            P("gx", "gy", "gz"),
            P(None, "gx", "gy", "gz"),
            P(("gx", "gy", "gz"), None, None, None),
            P(("gx", "gy", "gz")),
            P(("gx", "gy", "gz"), None),
        ),
        out_specs=(P(None, "gx", "gy", "gz"), P(None, "gx", "gy", "gz")),
        check_vma=False,
    )
```

```python
import functools

import jax
import jax.numpy as jnp
from jax import lax
from jax.experimental import pallas as pl
from jax.experimental.pallas import tpu as pltpu
from jax.sharding import PartitionSpec as P

ITERS = 2
CHEB = 2

RELAX_WEIGHT = 0.8
CENTRE_VALUE = 2.0
HALF_WIDTH = 1.0

MESH = pl.DeviceIdType.MESH
F32 = jnp.float32
BF16 = jnp.bfloat16


def flip(place, bits):
    bit = 1
    while bit <= bits:
        if bits & bit:
            place = place + bit - 2 * bit * ((place // bit) % 2)
        bit *= 2
    return place


def kernel(
    sizes,
    r_ref,
    s_ref,
    react_ref,
    z_ref,
    b_ref,
    owner_ref,
    near_ref,
    sol_ref,
    res_ref,
    cells_in,
    coef,
    wpad,
    smooth,
    blocks,
    owners,
    line0,
    line1,
    line2,
    line3,
    xsend,
    xrecv,
    ysend,
    yrecv,
    zsend,
    zrecv,
    owner_send_sem,
    owner_recv_sem,
    line_send_sem,
    line_recv_sem,
    face_send_sem,
    face_recv_sem,
    field_sem,
    cells_sem,
):
    n_gx, n_gy, n_gz, cx, cy, cz = sizes
    rows = res_ref.shape[0]
    n_chips = n_gz // 2
    pad_y = cy + 2
    a, b, g = lax.axis_index("gx"), lax.axis_index("gy"), lax.axis_index("gz")
    chip, core = g // 2, g % 2
    partner = chip * 2 + 1 - core
    line = (line0, line1, line2, line3)

    def at_line(place):
        return {"gz": place}

    def cells_copy(which, x):
        source = (s_ref, react_ref)[which]
        return pltpu.make_async_copy(
            source.at[x], cells_in.at[which, pl.ds(x * cy, cy), :], cells_sem.at[which, x]
        )

    def field_copy(x, y):
        return pltpu.make_async_copy(
            r_ref.at[:, x, y, :],
            res_ref.at[:, pl.ds((x * cy + y) * cz, cz)],
            field_sem.at[x, y],
        )

    for x in range(cx):
        for which in range(2):
            cells_copy(which, x).start()
    for x in range(cx):
        for y in range(cy):
            field_copy(x, y).start()

    barrier = pltpu.get_barrier_semaphore()
    for step in range(1, n_gz):
        pl.semaphore_signal(
            barrier, inc=1, device_id=at_line((g + step) % n_gz), device_id_type=MESH
        )
    places = (("gx", a, n_gx), ("gy", b, n_gy))
    for name, place, count in places:

        @pl.when(place > 0)
        def _():
            pl.semaphore_signal(
                barrier, inc=1, device_id={name: place - 1}, device_id_type=MESH
            )

        @pl.when(place < count - 1)
        def _():
            pl.semaphore_signal(
                barrier, inc=1, device_id={name: place + 1}, device_id_type=MESH
            )

    for x in range(cx):
        for which in range(2):
            cells_copy(which, x).wait()
    stiff = cells_in[0]
    diagonal = 6.0 * stiff * stiff + cells_in[1]
    relax = RELAX_WEIGHT / diagonal
    coef[0] = stiff
    coef[1] = diagonal
    coef[2] = (2.0 - RELAX_WEIGHT) * relax
    coef[3] = stiff * relax

    lane = lax.broadcasted_iota(jnp.int32, (rows, cz), 1)
    narrow = lax.broadcasted_iota(jnp.int32, (rows, 128), 1)

    def cols(j):
        return pl.ds(pl.multiple_of(j * cz, cz), cz)

    def padded(j):
        x, y = j // cy, j % cy
        return ((x + 1) * pad_y + y + 1) * cz

    def pcols(offset):
        return pl.ds(pl.multiple_of(offset, cz), cz)

    def row(which, j):
        return coef[which, pl.ds(j, 1), :]

    def beside(offset):
        centre = wpad[:, pcols(offset)]
        total = wpad[:, pcols(offset + pad_y * cz)] + wpad[:, pcols(offset - pad_y * cz)]
        total = total + wpad[:, pcols(offset + cz)] + wpad[:, pcols(offset - cz)]
        total = total + jnp.where(lane == cz - 1, 0.0, pltpu.roll(centre, cz - 1, 1))
        return total + jnp.where(lane == 0, 0.0, pltpu.roll(centre, 1, 1))

    def each(first, count, body):
        def step(i, carry):
            body(first + i)
            return carry

        lax.fori_loop(0, count, step, 0)

    def clear():
        zero_row = jnp.zeros((rows, pad_y * cz), F32)
        wpad[:, pl.ds(0, pad_y * cz)] = zero_row
        wpad[:, pl.ds((cx + 1) * pad_y * cz, pad_y * cz)] = zero_row
        for x in range(cx):
            wpad[:, pl.ds((x + 1) * pad_y * cz, cz)] = jnp.zeros((rows, cz), F32)
            wpad[:, pl.ds(((x + 2) * pad_y - 1) * cz, cz)] = jnp.zeros((rows, cz), F32)

        faces = (("gx", a, n_gx, xrecv), ("gy", b, n_gy, yrecv), ("gz", g, n_gz, zrecv))
        for it in range(ITERS):
            for name, place, count, recv in faces:

                @pl.when(place == 0)
                def _():
                    recv[it, 0] = jnp.zeros(recv.shape[2:], recv.dtype)

                @pl.when(place == count - 1)
                def _():
                    recv[it, 1] = jnp.zeros(recv.shape[2:], recv.dtype)

    width = cy * cz

    def restrict_layer(values, x):
        return lax.dot_general(
            values.astype(BF16),
            z_ref[:, pl.ds(pl.multiple_of(x * width, width), width)],
            (((1,), (1,)), ((), ())),
            preferred_element_type=F32,
        )

    def restrict(first):
        total = jnp.zeros((rows, z_ref.shape[0]), F32)
        for x in range(cx):
            if first:
                for y in range(cy):
                    field_copy(x, y).wait()
            total = total + restrict_layer(res_ref[:, pl.ds(x * width, width)], x)
        return total

    def line_copy(turn, slot, sem, target):
        return pltpu.make_async_remote_copy(
            src_ref=line[turn].at[slot],
            dst_ref=line[turn].at[slot],
            send_sem=line_send_sem.at[turn, sem],
            recv_sem=line_recv_sem.at[turn, slot],
            device_id=at_line(target),
            device_id_type=MESH,
        )

    def line_start(turn, value):
        line[turn][g] = value
        for bits in range(n_chips - 1, 0, -1):
            line_copy(turn, g, bits, flip(chip, bits) * 2 + core).start()
        line_copy(turn, g, 0, partner).start()

    def line_finish(turn):
        for bits in range(1, n_chips):
            source = flip(chip, bits) * 2 + core
            line_copy(turn, source, 0, partner).wait_recv()
            line_copy(turn, source, n_chips + bits, partner).start()
        line_copy(turn, partner, 0, partner).wait_recv()
        for bits in range(1, n_chips):
            source = flip(chip, bits) * 2 + 1 - core
            line_copy(turn, source, 0, partner).wait_recv()

    def line_drain(turn):
        for sem in range(n_chips):
            line_copy(turn, g, sem, partner).wait_send()
        for bits in range(1, n_chips):
            line_copy(turn, g, n_chips + bits, partner).wait_send()

    def face_copy(it, axis, side, send, recv, name, target):
        return pltpu.make_async_remote_copy(
            src_ref=send.at[it, side],
            dst_ref=recv.at[it, 1 - side],
            send_sem=face_send_sem.at[it, axis, side],
            recv_sem=face_recv_sem.at[it, axis, 1 - side],
            device_id={name: target},
            device_id_type=MESH,
        )

    exchange = (
        (0, "gx", a, n_gx, xsend, xrecv),
        (1, "gy", b, n_gy, ysend, yrecv),
        (2, "gz", g, n_gz, zsend, zrecv),
    )

    def face_start(it, which, side):
        axis, name, place, count, send, recv = exchange[which]
        target = place - 1 + 2 * side

        @pl.when((target >= 0) & (target < count))
        def _():
            face_copy(it, axis, side, send, recv, name, target).start()

    def face_wait(it, which, side):
        axis, name, place, count, send, recv = exchange[which]
        source = place - 1 + 2 * side

        @pl.when((source >= 0) & (source < count))
        def _():
            face_copy(it, axis, 1 - side, send, recv, name, source).wait_recv()

    def face_drain(it, which):
        axis, name, place, count, send, recv = exchange[which]

        @pl.when(place > 0)
        def _():
            face_copy(it, axis, 0, send, recv, name, place - 1).wait_send()

        @pl.when(place < count - 1)
        def _():
            face_copy(it, axis, 1, send, recv, name, place + 1).wait_send()

    def relaxed(field):
        def scale(j):
            wpad[:, pcols(padded(j))] = row(3, j) * field[:, cols(j)]

        def combine(j):
            smooth[:, cols(j)] = row(2, j) * field[:, cols(j)] + row(3, j) * beside(padded(j))

        each(0, cx * cy, scale)
        each(0, cx * cy, combine)

    def apply_coarse(turn, value):
        picked = [value] + [line[turn][near_ref[0, k]] for k in range(6)]
        return jnp.dot(
            jnp.concatenate(picked, axis=1), blocks[...], preferred_element_type=F32
        )

    def owner_copy(target):
        return pltpu.make_async_remote_copy(
            src_ref=owners.at[g],
            dst_ref=owners.at[g],
            send_sem=owner_send_sem,
            recv_sem=owner_recv_sem,
            device_id=at_line(target),
            device_id_type=MESH,
        )

    owners[g] = jnp.full((1, 128), owner_ref[0], jnp.int32)
    for it in range(ITERS):
        field = res_ref
        if it == 0:
            coarse_rhs = restrict(True)
        coarse_rhs = coarse_rhs.astype(BF16)
        if it == 0:
            peers = n_gz - 1
            for name, place, count in places:
                for way in (place, count - 1 - place):
                    peers = peers + (way + count - 1) // count
            pl.semaphore_wait(barrier, peers)
            for step in range(1, n_gz):
                owner_copy((g + step) % n_gz).start()
        line_start(CHEB * it, coarse_rhs)
        if it == 0:
            clear()
        relaxed(field)
        if it == 0:
            others = owners.at[pl.ds(0, n_gz - 1)]
            pltpu.make_async_copy(others, others, owner_recv_sem).wait()
            blocks[pl.ds(0, 128), :] = b_ref[pl.ds(0, 128), :]
            for k in range(6):
                keep = owners[near_ref[0, k]] == owner_ref[0]
                part = pl.ds((k + 1) * 128, 128)
                blocks[part, :] = jnp.where(keep, b_ref[part, :].astype(F32), 0.0).astype(BF16)

        target = coarse_rhs.astype(F32)
        ratio_now = HALF_WIDTH / CENTRE_VALUE
        direction = target / CENTRE_VALUE
        coarse = direction
        for step in range(CHEB):
            ratio_next = 1.0 / (2.0 * CENTRE_VALUE / HALF_WIDTH - ratio_now)
            turn = CHEB * it + step
            line_finish(turn)
            if step == 0:
                misfit = target - apply_coarse(turn, coarse_rhs) / CENTRE_VALUE
            else:
                misfit = target - apply_coarse(turn, coarse.astype(BF16))
            direction = (
                ratio_next * ratio_now * direction + 2.0 * ratio_next / HALF_WIDTH * misfit
            )
            coarse = coarse + direction
            ratio_now = ratio_next
            if step < CHEB - 1:
                line_start(turn + 1, coarse.astype(BF16))
        coarse = coarse.astype(BF16)

        def correct(j):
            update = smooth[:, cols(j)] + jnp.dot(
                coarse, z_ref[:, cols(j)], preferred_element_type=F32
            )
            smooth[:, cols(j)] = update
            scaled = row(0, j) * update
            wpad[:, pcols(padded(j))] = scaled
            if it == 0:
                sol_ref[:, cols(j)] = update
            else:
                sol_ref[:, cols(j)] = sol_ref[:, cols(j)] + update
            return scaled

        sides = (a % 2, 1 - a % 2)
        for side in sides:

            def correct_layer(y):
                scaled = correct(side * ((cx - 1) * cy) + y)
                xsend[it, side, :, cols(y)] = scaled.astype(BF16)

            each(0, cy, correct_layer)
            face_start(it, 0, side)
        each(cy, (cx - 2) * cy, correct)
        for side, y in enumerate((0, cy - 1)):
            for x in range(cx):
                ysend[it, side, :, pl.ds(x * cz, cz)] = wpad[
                    :, pl.ds(((x + 1) * pad_y + y + 1) * cz, cz)
                ].astype(BF16)
            face_start(it, 1, side)

        def gather(j, carry):
            low, high = carry
            first = wpad[:, pl.ds(pl.multiple_of(padded(j), 128), 128)]
            last = wpad[:, pl.ds(pl.multiple_of(padded(j) + cz - 128, 128), 128)]
            low = jnp.where(narrow == j, pltpu.roll(first, j, 1), low)
            high = jnp.where(narrow == j, pltpu.roll(last, j + 1, 1), high)
            return low, high

        empty = jnp.zeros((rows, 128), F32)
        low, high = lax.fori_loop(0, cx * cy, gather, (empty, empty))
        zsend[it, 0] = low.astype(BF16)
        zsend[it, 1] = high.astype(BF16)
        face_start(it, 2, 0)
        face_start(it, 2, 1)

        def apply_inside(j):
            res_ref[:, cols(j)] = (
                field[:, cols(j)]
                - row(1, j) * smooth[:, cols(j)]
                + row(0, j) * beside(padded(j))
            )

        each(0, cx * cy, apply_inside)

        face_wait(it, 2, 0)
        face_wait(it, 2, 1)
        zlow, zhigh = zrecv[it, 0].astype(F32), zrecv[it, 1].astype(F32)

        def add_z(j):
            first = pl.ds(pl.multiple_of(j * cz, 128), 128)
            last = pl.ds(pl.multiple_of(j * cz + cz - 128, 128), 128)
            scale = coef[0, pl.ds(j, 1), :]
            res_ref[:, first] = res_ref[:, first] + jnp.where(
                narrow == 0, scale[:, :128] * pltpu.roll(zlow, (128 - j) % 128, 1), 0.0
            )
            res_ref[:, last] = res_ref[:, last] + jnp.where(
                narrow == 127, scale[:, cz - 128 :] * pltpu.roll(zhigh, 127 - j, 1), 0.0
            )

        each(0, cx * cy, add_z)
        for side, y in enumerate((0, cy - 1)):
            face_wait(it, 1, side)
            for x in range(cx):
                j = x * cy + y
                part = pl.ds(j * cz, cz)
                res_ref[:, part] = res_ref[:, part] + coef[0, pl.ds(j, 1), :] * yrecv[
                    it, side, :, pl.ds(x * cz, cz)
                ].astype(F32)
        for turn, side in enumerate((1 - a % 2, a % 2)):
            if turn == 1 and it < ITERS - 1:
                coarse_rhs = restrict(False)
            face_wait(it, 0, side)
            x = side * (cx - 1)
            terms = []
            for y in range(cy):
                j = x * cy + y
                term = row(0, j) * xrecv[it, side, :, pl.ds(y * cz, cz)].astype(F32)
                res_ref[:, cols(j)] = res_ref[:, cols(j)] + term
                terms.append(term.astype(BF16))
            if turn == 1 and it < ITERS - 1:
                coarse_rhs = coarse_rhs + restrict_layer(jnp.concatenate(terms, axis=1), x)

    for it in range(ITERS):
        for step in range(CHEB):
            line_drain(CHEB * it + step)
        for which in range(3):
            face_drain(it, which)
    others = owners.at[pl.ds(0, n_gz - 1)]
    pltpu.make_async_copy(others, others, owner_send_sem).wait()


def emit(sol_ref, res_ref, sol_out, res_out, sem):
    rows, cx, cy, cz = sol_out.shape
    copies = []
    for which, (source, target) in enumerate(((sol_ref, sol_out), (res_ref, res_out))):
        for x in range(cx):
            for y in range(cy):
                copies.append(
                    pltpu.make_async_copy(
                        source.at[:, pl.ds((x * cy + y) * cz, cz)],
                        target.at[:, x, y, :],
                        sem.at[which, x, y],
                    )
                )
    for copy in copies:
        copy.start()
    for copy in copies:
        copy.wait()


def local(sizes, right_side, stiffness, reaction, deflation, coarse_blocks, row_owner, neighbours):
    n_gx, n_gy, n_gz = sizes
    rows, cx, cy, cz = right_side.shape
    cells = cx * cy * cz
    vectors = deflation.shape[0]
    vmem = pl.BlockSpec(memory_space=pltpu.VMEM)
    smem = pl.BlockSpec(memory_space=pltpu.SMEM)
    hbm = pl.BlockSpec(memory_space=pl.ANY)
    turns = ITERS * CHEB
    flat = jax.ShapeDtypeStruct((rows, cells), F32)
    solution, residual = pl.pallas_call(
        functools.partial(kernel, (n_gx, n_gy, n_gz, cx, cy, cz)),
        out_shape=(flat, flat),
        in_specs=[hbm] * 3 + [vmem] * 2 + [smem] * 2,
        out_specs=(vmem, vmem),
        scratch_shapes=[
            pltpu.VMEM((2, cx * cy, cz), F32),
            pltpu.VMEM((4, cx * cy, cz), F32),
            pltpu.VMEM((rows, (cx + 2) * (cy + 2) * cz), F32),
            pltpu.VMEM((rows, cells), F32),
            pltpu.VMEM((7 * vectors, vectors), BF16),
            pltpu.VMEM((n_gz, 1, 128), jnp.int32),
            *[pltpu.VMEM((n_gz, rows, vectors), BF16)] * turns,
            pltpu.VMEM((ITERS, 2, rows, cy * cz), BF16),
            pltpu.VMEM((ITERS, 2, rows, cy * cz), BF16),
            pltpu.VMEM((ITERS, 2, rows, cx * cz), BF16),
            pltpu.VMEM((ITERS, 2, rows, cx * cz), BF16),
            pltpu.VMEM((ITERS, 2, rows, 128), BF16),
            pltpu.VMEM((ITERS, 2, rows, 128), BF16),
            pltpu.SemaphoreType.DMA,
            pltpu.SemaphoreType.DMA,
            pltpu.SemaphoreType.DMA((turns, n_gz)),
            pltpu.SemaphoreType.DMA((turns, n_gz)),
            pltpu.SemaphoreType.DMA((ITERS, 3, 2)),
            pltpu.SemaphoreType.DMA((ITERS, 3, 2)),
            pltpu.SemaphoreType.DMA((cx, cy)),
            pltpu.SemaphoreType.DMA((2, cx)),
        ],
        compiler_params=pltpu.CompilerParams(
            collective_id=0, has_side_effects=True, vmem_limit_bytes=28 * 1024 * 1024
        ),
        name="schwarz",
    )(
        right_side,
        stiffness,
        reaction,
        deflation.reshape(vectors, cells),
        coarse_blocks.reshape(7 * vectors, vectors),
        row_owner,
        neighbours,
    )
    whole = jax.ShapeDtypeStruct(right_side.shape, F32)
    return pl.pallas_call(
        emit,
        out_shape=(whole, whole),
        in_specs=[vmem, vmem],
        out_specs=(hbm, hbm),
        scratch_shapes=[pltpu.SemaphoreType.DMA((2, cx, cy))],
        compiler_params=pltpu.CompilerParams(vmem_limit_bytes=4 * 1024 * 1024),
        name="emit",
    )(solution, residual)


def solution(mesh):
    sizes = tuple(mesh.shape[name] for name in ("gx", "gy", "gz"))
    return jax.shard_map(
        functools.partial(local, sizes),
        mesh=mesh,
        in_specs=(
            P(None, "gx", "gy", "gz"),
            P("gx", "gy", "gz"),
            P("gx", "gy", "gz"),
            P(None, "gx", "gy", "gz"),
            P(("gx", "gy", "gz"), None, None, None),
            P(("gx", "gy", "gz")),
            P(("gx", "gy", "gz"), None),
        ),
        out_specs=(P(None, "gx", "gy", "gz"), P(None, "gx", "gy", "gz")),
        check_vma=False,
    )
```

```python
import functools

import jax
import jax.numpy as jnp
from jax import lax
from jax.experimental import pallas as pl
from jax.experimental.pallas import tpu as pltpu
from jax.sharding import PartitionSpec as P

ITERS = 2
CHEB = 2

RELAX_WEIGHT = 0.8
CENTRE_VALUE = 2.0
HALF_WIDTH = 1.0

STRAIGHT = 640

MESH = pl.DeviceIdType.MESH
F32 = jnp.float32
BF16 = jnp.bfloat16


def flip(place, bits):
    bit = 1
    while bit <= bits:
        if bits & bit:
            place = place + bit - 2 * bit * ((place // bit) % 2)
        bit *= 2
    return place


def kernel(
    sizes,
    r_ref,
    s_ref,
    react_ref,
    z_ref,
    b_ref,
    owner_ref,
    near_ref,
    sol_ref,
    res_ref,
    cells_in,
    coef,
    wpad,
    smooth,
    blocks,
    owners,
    line0,
    line1,
    line2,
    line3,
    xsend,
    xrecv,
    ysend,
    yrecv,
    zsend,
    zrecv,
    owner_send_sem,
    owner_recv_sem,
    line_send_sem,
    line_recv_sem,
    face_send_sem,
    face_recv_sem,
    field_sem,
    cells_sem,
    around,
    around_send_sem,
    around_recv_sem,
):
    n_gx, n_gy, n_gz, cx, cy, cz = sizes
    rows = res_ref.shape[0]
    n_chips = n_gz // 2
    pad_y = cy + 2
    a, b, g = lax.axis_index("gx"), lax.axis_index("gy"), lax.axis_index("gz")
    chip, core = g // 2, g % 2
    partner = chip * 2 + 1 - core
    line = (line0, line1, line2, line3)

    def at_line(place):
        return {"gz": place}

    half = n_gx // 2
    low_far, high_far = half - 1, half
    is_far = (a - low_far) * (a - high_far) == 0
    is_edge = a * (a - (n_gx - 1)) == 0

    def cells_copy(which, x):
        source = (s_ref, react_ref)[which]
        return pltpu.make_async_copy(
            source.at[x], cells_in.at[which, pl.ds(x * cy, cy), :], cells_sem.at[which, x]
        )

    def field_copy(x, y):
        return pltpu.make_async_copy(
            r_ref.at[:, x, y, :],
            res_ref.at[:, pl.ds((x * cy + y) * cz, cz)],
            field_sem.at[x, y],
        )

    for x in range(cx):
        for which in range(2):
            cells_copy(which, x).start()
    for x in range(cx):
        for y in range(cy):
            field_copy(x, y).start()

    barrier = pltpu.get_barrier_semaphore()
    for step in range(1, n_gz):
        pl.semaphore_signal(
            barrier, inc=1, device_id=at_line((g + step) % n_gz), device_id_type=MESH
        )
    places = (("gx", a, n_gx), ("gy", b, n_gy))
    for name, place, count in places:

        @pl.when(place > 0)
        def _():
            pl.semaphore_signal(
                barrier, inc=1, device_id={name: place - 1}, device_id_type=MESH
            )

        @pl.when(place < count - 1)
        def _():
            pl.semaphore_signal(
                barrier, inc=1, device_id={name: place + 1}, device_id_type=MESH
            )

    for here, others in ((is_far, (0, n_gx - 1)), (is_edge, (low_far, high_far))):

        @pl.when(here)
        def _():
            for other in others:
                pl.semaphore_signal(
                    barrier, inc=1, device_id={"gx": other}, device_id_type=MESH
                )

    for x in range(cx):
        for which in range(2):
            cells_copy(which, x).wait()
    stiff = cells_in[0]
    diagonal = 6.0 * stiff * stiff + cells_in[1]
    relax = RELAX_WEIGHT / diagonal
    coef[0] = stiff
    coef[1] = diagonal
    coef[2] = (2.0 - RELAX_WEIGHT) * relax
    coef[3] = stiff * relax

    lane = lax.broadcasted_iota(jnp.int32, (rows, cz), 1)
    narrow = lax.broadcasted_iota(jnp.int32, (rows, 128), 1)

    def cols(j):
        return pl.ds(pl.multiple_of(j * cz, cz), cz)

    def padded(j):
        x, y = j // cy, j % cy
        return ((x + 1) * pad_y + y + 1) * cz

    def pcols(offset):
        return pl.ds(pl.multiple_of(offset, cz), cz)

    def row(which, j):
        return coef[which, pl.ds(j, 1), :]

    def beside(offset):
        centre = wpad[:, pcols(offset)]
        total = wpad[:, pcols(offset + pad_y * cz)] + wpad[:, pcols(offset - pad_y * cz)]
        total = total + wpad[:, pcols(offset + cz)] + wpad[:, pcols(offset - cz)]
        total = total + jnp.where(lane == cz - 1, 0.0, pltpu.roll(centre, cz - 1, 1))
        return total + jnp.where(lane == 0, 0.0, pltpu.roll(centre, 1, 1))

    def each(first, count, body):
        def step(i, carry):
            body(first + i)
            return carry

        lax.fori_loop(0, count, step, 0)

    def clear():
        zero_row = jnp.zeros((rows, pad_y * cz), F32)
        wpad[:, pl.ds(0, pad_y * cz)] = zero_row
        wpad[:, pl.ds((cx + 1) * pad_y * cz, pad_y * cz)] = zero_row
        for x in range(cx):
            wpad[:, pl.ds((x + 1) * pad_y * cz, cz)] = jnp.zeros((rows, cz), F32)
            wpad[:, pl.ds(((x + 2) * pad_y - 1) * cz, cz)] = jnp.zeros((rows, cz), F32)

        faces = (("gx", a, n_gx, xrecv), ("gy", b, n_gy, yrecv), ("gz", g, n_gz, zrecv))
        for it in range(ITERS):
            for name, place, count, recv in faces:

                @pl.when(place == 0)
                def _():
                    recv[it, 0] = jnp.zeros(recv.shape[2:], recv.dtype)

                @pl.when(place == count - 1)
                def _():
                    recv[it, 1] = jnp.zeros(recv.shape[2:], recv.dtype)

    width = cy * cz

    def restrict_layer(values, x):
        return lax.dot_general(
            values.astype(BF16),
            z_ref[:, pl.ds(pl.multiple_of(x * width, width), width)],
            (((1,), (1,)), ((), ())),
            preferred_element_type=F32,
        )

    def restrict(first):
        total = jnp.zeros((rows, z_ref.shape[0]), F32)
        for x in range(cx):
            if first:
                for y in range(cy):
                    field_copy(x, y).wait()
            total = total + restrict_layer(res_ref[:, pl.ds(x * width, width)], x)
        return total

    def line_copy(turn, slot, sem, target):
        return pltpu.make_async_remote_copy(
            src_ref=line[turn].at[slot],
            dst_ref=line[turn].at[slot],
            send_sem=line_send_sem.at[turn, sem],
            recv_sem=line_recv_sem.at[turn, slot],
            device_id=at_line(target),
            device_id_type=MESH,
        )

    def line_start(turn, value):
        line[turn][g] = value
        for bits in range(n_chips - 1, 0, -1):
            line_copy(turn, g, bits, flip(chip, bits) * 2 + core).start()
        line_copy(turn, g, 0, partner).start()

    def line_finish(turn):
        for bits in range(1, n_chips):
            source = flip(chip, bits) * 2 + core
            line_copy(turn, source, 0, partner).wait_recv()
            line_copy(turn, source, n_chips + bits, partner).start()
        line_copy(turn, partner, 0, partner).wait_recv()
        for bits in range(1, n_chips):
            source = flip(chip, bits) * 2 + 1 - core
            line_copy(turn, source, 0, partner).wait_recv()

    def line_drain(turn):
        for sem in range(n_chips):
            line_copy(turn, g, sem, partner).wait_send()
        for bits in range(1, n_chips):
            line_copy(turn, g, n_chips + bits, partner).wait_send()

    def face_copy(it, axis, side, send, recv, name, target):
        return pltpu.make_async_remote_copy(
            src_ref=send.at[it, side],
            dst_ref=recv.at[it, 1 - side],
            send_sem=face_send_sem.at[it, axis, side],
            recv_sem=face_recv_sem.at[it, axis, 1 - side],
            device_id={name: target},
            device_id_type=MESH,
        )

    exchange = (
        (0, "gx", a, n_gx, xsend, xrecv),
        (1, "gy", b, n_gy, ysend, yrecv),
        (2, "gz", g, n_gz, zsend, zrecv),
    )

    def touches(which, place, side, other, count):
        inside = (other >= 0) & (other < count)
        if which == 0:
            inside = inside & (place + other != low_far + high_far)
        return inside

    def face_start(it, which, side):
        axis, name, place, count, send, recv = exchange[which]
        target = place - 1 + 2 * side

        @pl.when(touches(which, place, side, target, count))
        def _():
            face_copy(it, axis, side, send, recv, name, target).start()

    def face_wait(it, which, side):
        axis, name, place, count, send, recv = exchange[which]
        source = place - 1 + 2 * side

        @pl.when(touches(which, place, side, source, count))
        def _():
            face_copy(it, axis, 1 - side, send, recv, name, source).wait_recv()

    straight = pl.ds(0, STRAIGHT)
    detour = pl.ds(STRAIGHT, cy * cz - STRAIGHT)
    far_side = a % 2
    far_place = low_far + high_far - a

    def straight_copy(it):
        return pltpu.make_async_remote_copy(
            src_ref=xsend.at[it, far_side, :, straight],
            dst_ref=xrecv.at[it, 1 - far_side, :, straight],
            send_sem=face_send_sem.at[it, 0, far_side],
            recv_sem=face_recv_sem.at[it, 0, 1 - far_side],
            device_id={"gx": far_place},
            device_id_type=MESH,
        )

    def out_copy(it):
        return pltpu.make_async_remote_copy(
            src_ref=xsend.at[it, far_side, :, detour],
            dst_ref=around.at[it],
            send_sem=around_send_sem.at[it, 0],
            recv_sem=around_recv_sem.at[it, 0],
            device_id={"gx": (1 - far_side) * (n_gx - 1)},
            device_id_type=MESH,
        )

    def on_copy(it, side, target):
        return pltpu.make_async_remote_copy(
            src_ref=around.at[it],
            dst_ref=xrecv.at[it, side, :, detour],
            send_sem=around_send_sem.at[it, 1],
            recv_sem=around_recv_sem.at[it, 1],
            device_id={"gx": target},
            device_id_type=MESH,
        )

    def far_start(it):
        @pl.when(is_far)
        def _():
            out_copy(it).start()
            straight_copy(it).start()

    def far_forward(it):
        @pl.when(is_edge)
        def _():
            out_copy(it).wait_recv()
            on_copy(it, a // (n_gx - 1), high_far - a // (n_gx - 1)).start()

    def far_wait(it):
        @pl.when(is_far)
        def _():
            pltpu.make_async_remote_copy(
                src_ref=xsend.at[it, far_side, :, straight],
                dst_ref=xrecv.at[it, far_side, :, straight],
                send_sem=face_send_sem.at[it, 0, far_side],
                recv_sem=face_recv_sem.at[it, 0, far_side],
                device_id={"gx": far_place},
                device_id_type=MESH,
            ).wait_recv()
            on_copy(it, far_side, far_place).wait_recv()

    def far_drain(it):
        @pl.when(is_far)
        def _():
            straight_copy(it).wait_send()
            out_copy(it).wait_send()

        @pl.when(is_edge)
        def _():
            on_copy(it, 1, low_far).wait_send()

    def face_drain(it, which):
        axis, name, place, count, send, recv = exchange[which]
        for side in range(2):
            target = place - 1 + 2 * side

            @pl.when(touches(which, place, side, target, count))
            def _():
                face_copy(it, axis, side, send, recv, name, target).wait_send()

    def relaxed(field):
        def scale(j):
            wpad[:, pcols(padded(j))] = row(3, j) * field[:, cols(j)]

        def combine(j):
            smooth[:, cols(j)] = row(2, j) * field[:, cols(j)] + row(3, j) * beside(padded(j))

        each(0, cx * cy, scale)
        each(0, cx * cy, combine)

    def apply_coarse(turn, value):
        picked = [value] + [line[turn][near_ref[0, k]] for k in range(6)]
        return jnp.dot(
            jnp.concatenate(picked, axis=1), blocks[...], preferred_element_type=F32
        )

    def owner_copy(target):
        return pltpu.make_async_remote_copy(
            src_ref=owners.at[g],
            dst_ref=owners.at[g],
            send_sem=owner_send_sem,
            recv_sem=owner_recv_sem,
            device_id=at_line(target),
            device_id_type=MESH,
        )

    owners[g] = jnp.full((1, 128), owner_ref[0], jnp.int32)
    for it in range(ITERS):
        field = res_ref
        if it == 0:
            coarse_rhs = restrict(True)
        coarse_rhs = coarse_rhs.astype(BF16)
        if it == 0:
            peers = n_gz - 1
            for name, place, count in places:
                for way in (place, count - 1 - place):
                    peers = peers + (way + count - 1) // count
            within = a % half
            for way in (within, half - 1 - within):
                peers = peers + 2 * (1 - (way + half - 1) // half)
            pl.semaphore_wait(barrier, peers)
            for step in range(1, n_gz):
                owner_copy((g + step) % n_gz).start()
        line_start(CHEB * it, coarse_rhs)
        if it == 0:
            clear()
        relaxed(field)
        if it == 0:
            others = owners.at[pl.ds(0, n_gz - 1)]
            pltpu.make_async_copy(others, others, owner_recv_sem).wait()
            blocks[pl.ds(0, 128), :] = b_ref[pl.ds(0, 128), :]
            for k in range(6):
                keep = owners[near_ref[0, k]] == owner_ref[0]
                part = pl.ds((k + 1) * 128, 128)
                blocks[part, :] = jnp.where(keep, b_ref[part, :].astype(F32), 0.0).astype(BF16)

        target = coarse_rhs.astype(F32)
        ratio_now = HALF_WIDTH / CENTRE_VALUE
        direction = target / CENTRE_VALUE
        coarse = direction
        for step in range(CHEB):
            ratio_next = 1.0 / (2.0 * CENTRE_VALUE / HALF_WIDTH - ratio_now)
            turn = CHEB * it + step
            line_finish(turn)
            if step == 0:
                misfit = target - apply_coarse(turn, coarse_rhs) / CENTRE_VALUE
            else:
                misfit = target - apply_coarse(turn, coarse.astype(BF16))
            direction = (
                ratio_next * ratio_now * direction + 2.0 * ratio_next / HALF_WIDTH * misfit
            )
            coarse = coarse + direction
            ratio_now = ratio_next
            if step < CHEB - 1:
                line_start(turn + 1, coarse.astype(BF16))
        coarse = coarse.astype(BF16)

        def correct(j):
            update = smooth[:, cols(j)] + jnp.dot(
                coarse, z_ref[:, cols(j)], preferred_element_type=F32
            )
            smooth[:, cols(j)] = update
            scaled = row(0, j) * update
            wpad[:, pcols(padded(j))] = scaled
            if it == 0:
                sol_ref[:, cols(j)] = update
            else:
                sol_ref[:, cols(j)] = sol_ref[:, cols(j)] + update
            return scaled

        sides = (a % 2, 1 - a % 2)
        for turn, side in enumerate(sides):

            def correct_layer(y):
                scaled = correct(side * ((cx - 1) * cy) + y)
                xsend[it, side, :, cols(y)] = scaled.astype(BF16)

            each(0, cy, correct_layer)
            face_start(it, 0, side)
            if turn == 0:
                far_start(it)
        each(cy, (cx - 2) * cy, correct)
        far_forward(it)
        for side, y in enumerate((0, cy - 1)):
            for x in range(cx):
                ysend[it, side, :, pl.ds(x * cz, cz)] = wpad[
                    :, pl.ds(((x + 1) * pad_y + y + 1) * cz, cz)
                ].astype(BF16)
            face_start(it, 1, side)

        def gather(j, carry):
            low, high = carry
            first = wpad[:, pl.ds(pl.multiple_of(padded(j), 128), 128)]
            last = wpad[:, pl.ds(pl.multiple_of(padded(j) + cz - 128, 128), 128)]
            low = jnp.where(narrow == j, pltpu.roll(first, j, 1), low)
            high = jnp.where(narrow == j, pltpu.roll(last, j + 1, 1), high)
            return low, high

        empty = jnp.zeros((rows, 128), F32)
        low, high = lax.fori_loop(0, cx * cy, gather, (empty, empty))
        zsend[it, 0] = low.astype(BF16)
        zsend[it, 1] = high.astype(BF16)
        face_start(it, 2, 0)
        face_start(it, 2, 1)

        def apply_inside(j):
            res_ref[:, cols(j)] = (
                field[:, cols(j)]
                - row(1, j) * smooth[:, cols(j)]
                + row(0, j) * beside(padded(j))
            )

        each(0, cx * cy, apply_inside)

        face_wait(it, 2, 0)
        face_wait(it, 2, 1)
        zlow, zhigh = zrecv[it, 0].astype(F32), zrecv[it, 1].astype(F32)

        def add_z(j):
            first = pl.ds(pl.multiple_of(j * cz, 128), 128)
            last = pl.ds(pl.multiple_of(j * cz + cz - 128, 128), 128)
            scale = coef[0, pl.ds(j, 1), :]
            res_ref[:, first] = res_ref[:, first] + jnp.where(
                narrow == 0, scale[:, :128] * pltpu.roll(zlow, (128 - j) % 128, 1), 0.0
            )
            res_ref[:, last] = res_ref[:, last] + jnp.where(
                narrow == 127, scale[:, cz - 128 :] * pltpu.roll(zhigh, 127 - j, 1), 0.0
            )

        each(0, cx * cy, add_z)
        for side, y in enumerate((0, cy - 1)):
            face_wait(it, 1, side)
            for x in range(cx):
                j = x * cy + y
                part = pl.ds(j * cz, cz)
                res_ref[:, part] = res_ref[:, part] + coef[0, pl.ds(j, 1), :] * yrecv[
                    it, side, :, pl.ds(x * cz, cz)
                ].astype(F32)
        for turn, side in enumerate((1 - a % 2, a % 2)):
            if turn == 1 and it < ITERS - 1:
                coarse_rhs = restrict(False)
            face_wait(it, 0, side)
            if turn == 1:
                far_wait(it)
            x = side * (cx - 1)
            terms = []
            for y in range(cy):
                j = x * cy + y
                term = row(0, j) * xrecv[it, side, :, pl.ds(y * cz, cz)].astype(F32)
                res_ref[:, cols(j)] = res_ref[:, cols(j)] + term
                terms.append(term.astype(BF16))
            if turn == 1 and it < ITERS - 1:
                coarse_rhs = coarse_rhs + restrict_layer(jnp.concatenate(terms, axis=1), x)

    for it in range(ITERS):
        far_drain(it)
        for step in range(CHEB):
            line_drain(CHEB * it + step)
        for which in range(3):
            face_drain(it, which)
    others = owners.at[pl.ds(0, n_gz - 1)]
    pltpu.make_async_copy(others, others, owner_send_sem).wait()


def emit(sol_ref, res_ref, sol_out, res_out, sem):
    rows, cx, cy, cz = sol_out.shape
    copies = []
    for which, (source, target) in enumerate(((sol_ref, sol_out), (res_ref, res_out))):
        for x in range(cx):
            for y in range(cy):
                copies.append(
                    pltpu.make_async_copy(
                        source.at[:, pl.ds((x * cy + y) * cz, cz)],
                        target.at[:, x, y, :],
                        sem.at[which, x, y],
                    )
                )
    for copy in copies:
        copy.start()
    for copy in copies:
        copy.wait()


def local(sizes, right_side, stiffness, reaction, deflation, coarse_blocks, row_owner, neighbours):
    n_gx, n_gy, n_gz = sizes
    rows, cx, cy, cz = right_side.shape
    cells = cx * cy * cz
    vectors = deflation.shape[0]
    vmem = pl.BlockSpec(memory_space=pltpu.VMEM)
    smem = pl.BlockSpec(memory_space=pltpu.SMEM)
    hbm = pl.BlockSpec(memory_space=pl.ANY)
    turns = ITERS * CHEB
    flat = jax.ShapeDtypeStruct((rows, cells), F32)
    solution, residual = pl.pallas_call(
        functools.partial(kernel, (n_gx, n_gy, n_gz, cx, cy, cz)),
        out_shape=(flat, flat),
        in_specs=[hbm] * 3 + [vmem] * 2 + [smem] * 2,
        out_specs=(vmem, vmem),
        scratch_shapes=[
            pltpu.VMEM((2, cx * cy, cz), F32),
            pltpu.VMEM((4, cx * cy, cz), F32),
            pltpu.VMEM((rows, (cx + 2) * (cy + 2) * cz), F32),
            pltpu.VMEM((rows, cells), F32),
            pltpu.VMEM((7 * vectors, vectors), BF16),
            pltpu.VMEM((n_gz, 1, 128), jnp.int32),
            *[pltpu.VMEM((n_gz, rows, vectors), BF16)] * turns,
            pltpu.VMEM((ITERS, 2, rows, cy * cz), BF16),
            pltpu.VMEM((ITERS, 2, rows, cy * cz), BF16),
            pltpu.VMEM((ITERS, 2, rows, cx * cz), BF16),
            pltpu.VMEM((ITERS, 2, rows, cx * cz), BF16),
            pltpu.VMEM((ITERS, 2, rows, 128), BF16),
            pltpu.VMEM((ITERS, 2, rows, 128), BF16),
            pltpu.SemaphoreType.DMA,
            pltpu.SemaphoreType.DMA,
            pltpu.SemaphoreType.DMA((turns, n_gz)),
            pltpu.SemaphoreType.DMA((turns, n_gz)),
            pltpu.SemaphoreType.DMA((ITERS, 3, 2)),
            pltpu.SemaphoreType.DMA((ITERS, 3, 2)),
            pltpu.SemaphoreType.DMA((cx, cy)),
            pltpu.SemaphoreType.DMA((2, cx)),
            pltpu.VMEM((ITERS, rows, cy * cz - STRAIGHT), BF16),
            pltpu.SemaphoreType.DMA((ITERS, 2)),
            pltpu.SemaphoreType.DMA((ITERS, 2)),
        ],
        compiler_params=pltpu.CompilerParams(
            collective_id=0, has_side_effects=True, vmem_limit_bytes=28 * 1024 * 1024
        ),
        name="schwarz",
    )(
        right_side,
        stiffness,
        reaction,
        deflation.reshape(vectors, cells),
        coarse_blocks.reshape(7 * vectors, vectors),
        row_owner,
        neighbours,
    )
    whole = jax.ShapeDtypeStruct(right_side.shape, F32)
    return pl.pallas_call(
        emit,
        out_shape=(whole, whole),
        in_specs=[vmem, vmem],
        out_specs=(hbm, hbm),
        scratch_shapes=[pltpu.SemaphoreType.DMA((2, cx, cy))],
        compiler_params=pltpu.CompilerParams(vmem_limit_bytes=4 * 1024 * 1024),
        name="emit",
    )(solution, residual)


def solution(mesh):
    sizes = tuple(mesh.shape[name] for name in ("gx", "gy", "gz"))
    return jax.shard_map(
        functools.partial(local, sizes),
        mesh=mesh,
        in_specs=(
            P(None, "gx", "gy", "gz"),
            P("gx", "gy", "gz"),
            P("gx", "gy", "gz"),
            P(None, "gx", "gy", "gz"),
            P(("gx", "gy", "gz"), None, None, None),
            P(("gx", "gy", "gz")),
            P(("gx", "gy", "gz"), None),
        ),
        out_specs=(P(None, "gx", "gy", "gz"), P(None, "gx", "gy", "gz")),
        check_vma=False,
    )
```

```python
import functools

import jax
import jax.numpy as jnp
from jax import lax
from jax.experimental import pallas as pl
from jax.experimental.pallas import tpu as pltpu
from jax.sharding import PartitionSpec as P

ITERS = 2
CHEB = 2

RELAX_WEIGHT = 0.8
CENTRE_VALUE = 2.0
HALF_WIDTH = 1.0

SHARES = (384, 128, 128)

MESH = pl.DeviceIdType.MESH
F32 = jnp.float32
BF16 = jnp.bfloat16


def flip(place, bits):
    bit = 1
    while bit <= bits:
        if bits & bit:
            place = place + bit - 2 * bit * ((place // bit) % 2)
        bit *= 2
    return place


def kernel(
    sizes,
    r_ref,
    s_ref,
    react_ref,
    z_ref,
    b_ref,
    owner_ref,
    near_ref,
    sol_ref,
    res_ref,
    cells_in,
    coef,
    wpad,
    smooth,
    blocks,
    owners,
    line0,
    line1,
    line2,
    line3,
    xsend,
    xrecv,
    ysend,
    yrecv,
    zsend,
    zrecv,
    owner_send_sem,
    owner_recv_sem,
    line_send_sem,
    line_recv_sem,
    face_send_sem,
    face_recv_sem,
    field_sem,
    cells_sem,
    around,
    around_send_sem,
    around_recv_sem,
):
    n_gx, n_gy, n_gz, cx, cy, cz = sizes
    rows = res_ref.shape[0]
    n_chips = n_gz // 2
    pad_y = cy + 2
    a, b, g = lax.axis_index("gx"), lax.axis_index("gy"), lax.axis_index("gz")
    chip, core = g // 2, g % 2
    partner = chip * 2 + 1 - core
    line = (line0, line1, line2, line3)

    def at_line(place):
        return {"gz": place}

    half = n_gx // 2
    low_far, high_far = half - 1, half
    apart = (a - low_far) * (a - high_far)
    is_far = apart == 0
    ways, start = [], cy * cz
    for via, share in zip([0, *range(half - 2, 0, -1)], SHARES):
        start -= share
        ways.append((via, pl.ds(start, share), share))
    straight = pl.ds(0, start)

    def cells_copy(which, x):
        source = (s_ref, react_ref)[which]
        return pltpu.make_async_copy(
            source.at[x], cells_in.at[which, pl.ds(x * cy, cy), :], cells_sem.at[which, x]
        )

    def field_copy(x, y):
        return pltpu.make_async_copy(
            r_ref.at[:, x, y, :],
            res_ref.at[:, pl.ds((x * cy + y) * cz, cz)],
            field_sem.at[x, y],
        )

    for x in range(cx):
        for which in range(2):
            cells_copy(which, x).start()
    for x in range(cx):
        for y in range(cy):
            field_copy(x, y).start()

    barrier = pltpu.get_barrier_semaphore()
    for step in range(1, n_gz):
        pl.semaphore_signal(
            barrier, inc=1, device_id=at_line((g + step) % n_gz), device_id_type=MESH
        )
    places = (("gx", a, n_gx), ("gy", b, n_gy))
    for name, place, count in places:

        @pl.when(place > 0)
        def _():
            pl.semaphore_signal(
                barrier, inc=1, device_id={name: place - 1}, device_id_type=MESH
            )

        @pl.when(place < count - 1)
        def _():
            pl.semaphore_signal(
                barrier, inc=1, device_id={name: place + 1}, device_id_type=MESH
            )

    @pl.when(is_far)
    def _():
        for other in [*range(low_far), *range(high_far + 1, n_gx)]:
            pl.semaphore_signal(
                barrier, inc=1, device_id={"gx": other}, device_id_type=MESH
            )

    @pl.when(apart > 0)
    def _():
        for other in (low_far, high_far):
            pl.semaphore_signal(
                barrier, inc=1, device_id={"gx": other}, device_id_type=MESH
            )

    for x in range(cx):
        for which in range(2):
            cells_copy(which, x).wait()
    stiff = cells_in[0]
    diagonal = 6.0 * stiff * stiff + cells_in[1]
    relax = RELAX_WEIGHT / diagonal
    coef[0] = stiff
    coef[1] = diagonal
    coef[2] = (2.0 - RELAX_WEIGHT) * relax
    coef[3] = stiff * relax

    lane = lax.broadcasted_iota(jnp.int32, (rows, cz), 1)
    narrow = lax.broadcasted_iota(jnp.int32, (rows, 128), 1)

    def cols(j):
        return pl.ds(pl.multiple_of(j * cz, cz), cz)

    def padded(j):
        x, y = j // cy, j % cy
        return ((x + 1) * pad_y + y + 1) * cz

    def pcols(offset):
        return pl.ds(pl.multiple_of(offset, cz), cz)

    def row(which, j):
        return coef[which, pl.ds(j, 1), :]

    def beside(offset):
        centre = wpad[:, pcols(offset)]
        total = wpad[:, pcols(offset + pad_y * cz)] + wpad[:, pcols(offset - pad_y * cz)]
        total = total + wpad[:, pcols(offset + cz)] + wpad[:, pcols(offset - cz)]
        total = total + jnp.where(lane == cz - 1, 0.0, pltpu.roll(centre, cz - 1, 1))
        return total + jnp.where(lane == 0, 0.0, pltpu.roll(centre, 1, 1))

    def each(first, count, body):
        def step(i, carry):
            body(first + i)
            return carry

        lax.fori_loop(0, count, step, 0)

    def clear():
        zero_row = jnp.zeros((rows, pad_y * cz), F32)
        wpad[:, pl.ds(0, pad_y * cz)] = zero_row
        wpad[:, pl.ds((cx + 1) * pad_y * cz, pad_y * cz)] = zero_row
        for x in range(cx):
            wpad[:, pl.ds((x + 1) * pad_y * cz, cz)] = jnp.zeros((rows, cz), F32)
            wpad[:, pl.ds(((x + 2) * pad_y - 1) * cz, cz)] = jnp.zeros((rows, cz), F32)

        faces = (("gx", a, n_gx, xrecv), ("gy", b, n_gy, yrecv), ("gz", g, n_gz, zrecv))
        for it in range(ITERS):
            for name, place, count, recv in faces:

                @pl.when(place == 0)
                def _():
                    recv[it, 0] = jnp.zeros(recv.shape[2:], recv.dtype)

                @pl.when(place == count - 1)
                def _():
                    recv[it, 1] = jnp.zeros(recv.shape[2:], recv.dtype)

    width = cy * cz

    def restrict_layer(values, x):
        return lax.dot_general(
            values.astype(BF16),
            z_ref[:, pl.ds(pl.multiple_of(x * width, width), width)],
            (((1,), (1,)), ((), ())),
            preferred_element_type=F32,
        )

    def restrict(first):
        total = jnp.zeros((rows, z_ref.shape[0]), F32)
        for x in range(cx):
            if first:
                for y in range(cy):
                    field_copy(x, y).wait()
            total = total + restrict_layer(res_ref[:, pl.ds(x * width, width)], x)
        return total

    def line_copy(turn, slot, sem, target):
        return pltpu.make_async_remote_copy(
            src_ref=line[turn].at[slot],
            dst_ref=line[turn].at[slot],
            send_sem=line_send_sem.at[turn, sem],
            recv_sem=line_recv_sem.at[turn, slot],
            device_id=at_line(target),
            device_id_type=MESH,
        )

    def line_start(turn, value):
        line[turn][g] = value
        for bits in range(n_chips - 1, 0, -1):
            line_copy(turn, g, bits, flip(chip, bits) * 2 + core).start()
        line_copy(turn, g, 0, partner).start()

    def line_finish(turn):
        for bits in range(1, n_chips):
            source = flip(chip, bits) * 2 + core
            line_copy(turn, source, 0, partner).wait_recv()
            line_copy(turn, source, n_chips + bits, partner).start()
        line_copy(turn, partner, 0, partner).wait_recv()
        for bits in range(1, n_chips):
            source = flip(chip, bits) * 2 + 1 - core
            line_copy(turn, source, 0, partner).wait_recv()

    def line_drain(turn):
        for sem in range(n_chips):
            line_copy(turn, g, sem, partner).wait_send()
        for bits in range(1, n_chips):
            line_copy(turn, g, n_chips + bits, partner).wait_send()

    def face_copy(it, axis, side, send, recv, name, target):
        return pltpu.make_async_remote_copy(
            src_ref=send.at[it, side],
            dst_ref=recv.at[it, 1 - side],
            send_sem=face_send_sem.at[it, axis, side],
            recv_sem=face_recv_sem.at[it, axis, 1 - side],
            device_id={name: target},
            device_id_type=MESH,
        )

    exchange = (
        (0, "gx", a, n_gx, xsend, xrecv),
        (1, "gy", b, n_gy, ysend, yrecv),
        (2, "gz", g, n_gz, zsend, zrecv),
    )

    def touches(which, place, side, other, count):
        inside = (other >= 0) & (other < count)
        if which == 0:
            inside = inside & (place + other != low_far + high_far)
        return inside

    def face_start(it, which, side):
        axis, name, place, count, send, recv = exchange[which]
        target = place - 1 + 2 * side

        @pl.when(touches(which, place, side, target, count))
        def _():
            face_copy(it, axis, side, send, recv, name, target).start()

    def face_wait(it, which, side):
        axis, name, place, count, send, recv = exchange[which]
        source = place - 1 + 2 * side

        @pl.when(touches(which, place, side, source, count))
        def _():
            face_copy(it, axis, 1 - side, send, recv, name, source).wait_recv()

    far_side = a % 2
    far_place = low_far + high_far - a

    def straight_copy(it, slot):
        return pltpu.make_async_remote_copy(
            src_ref=xsend.at[it, far_side, :, straight],
            dst_ref=xrecv.at[it, slot, :, straight],
            send_sem=face_send_sem.at[it, 0, far_side],
            recv_sem=face_recv_sem.at[it, 0, slot],
            device_id={"gx": far_place},
            device_id_type=MESH,
        )

    def out_copy(it, way):
        via, part, share = ways[way]
        return pltpu.make_async_remote_copy(
            src_ref=xsend.at[it, far_side, :, part],
            dst_ref=around.at[it, :, pl.ds(0, share)],
            send_sem=around_send_sem.at[it, 0, way],
            recv_sem=around_recv_sem.at[it, 0, way],
            device_id={"gx": via + (1 - far_side) * (n_gx - 1 - 2 * via)},
            device_id_type=MESH,
        )

    def on_copy(it, way, slot, target):
        via, part, share = ways[way]
        return pltpu.make_async_remote_copy(
            src_ref=around.at[it, :, pl.ds(0, share)],
            dst_ref=xrecv.at[it, slot, :, part],
            send_sem=around_send_sem.at[it, 1, way],
            recv_sem=around_recv_sem.at[it, 1, way],
            device_id={"gx": target},
            device_id_type=MESH,
        )

    def far_start(it):
        @pl.when(is_far)
        def _():
            for way in range(len(ways)):
                out_copy(it, way).start()
            straight_copy(it, 1 - far_side).start()

    def each_via(action):
        for way, (via, part, share) in enumerate(ways):

            @pl.when((a - via) * (a - (n_gx - 1 - via)) == 0)
            def _():
                action(way)

    def far_forward(it):
        def forward(way):
            out_copy(it, way).wait_recv()
            on_copy(it, way, a // half, high_far - a // half).start()

        each_via(forward)

    def far_wait(it):
        @pl.when(is_far)
        def _():
            straight_copy(it, far_side).wait_recv()
            for way in range(len(ways)):
                on_copy(it, way, far_side, far_place).wait_recv()

    def far_drain(it):
        @pl.when(is_far)
        def _():
            straight_copy(it, 1 - far_side).wait_send()
            for way in range(len(ways)):
                out_copy(it, way).wait_send()

        each_via(lambda way: on_copy(it, way, a // half, high_far - a // half).wait_send())

    def face_drain(it, which):
        axis, name, place, count, send, recv = exchange[which]
        for side in range(2):
            target = place - 1 + 2 * side

            @pl.when(touches(which, place, side, target, count))
            def _():
                face_copy(it, axis, side, send, recv, name, target).wait_send()

    def relaxed(field):
        def scale(j):
            wpad[:, pcols(padded(j))] = row(3, j) * field[:, cols(j)]

        def combine(j):
            smooth[:, cols(j)] = row(2, j) * field[:, cols(j)] + row(3, j) * beside(padded(j))

        each(0, cx * cy, scale)
        each(0, cx * cy, combine)

    def apply_coarse(turn, value):
        picked = [value] + [line[turn][near_ref[0, k]] for k in range(6)]
        return jnp.dot(
            jnp.concatenate(picked, axis=1), blocks[...], preferred_element_type=F32
        )

    def owner_copy(target):
        return pltpu.make_async_remote_copy(
            src_ref=owners.at[g],
            dst_ref=owners.at[g],
            send_sem=owner_send_sem,
            recv_sem=owner_recv_sem,
            device_id=at_line(target),
            device_id_type=MESH,
        )

    owners[g] = jnp.full((1, 128), owner_ref[0], jnp.int32)
    for it in range(ITERS):
        field = res_ref
        if it == 0:
            coarse_rhs = restrict(True)
        coarse_rhs = coarse_rhs.astype(BF16)
        if it == 0:
            peers = n_gz - 1
            for name, place, count in places:
                for way in (place, count - 1 - place):
                    peers = peers + (way + count - 1) // count
            most = n_gx * n_gx
            peers = peers + 2 + (n_gx - 4) * (1 - (apart + most - 1) // most)
            pl.semaphore_wait(barrier, peers)
            for step in range(1, n_gz):
                owner_copy((g + step) % n_gz).start()
        line_start(CHEB * it, coarse_rhs)
        if it == 0:
            clear()
        relaxed(field)
        if it == 0:
            others = owners.at[pl.ds(0, n_gz - 1)]
            pltpu.make_async_copy(others, others, owner_recv_sem).wait()
            blocks[pl.ds(0, 128), :] = b_ref[pl.ds(0, 128), :]
            for k in range(6):
                keep = owners[near_ref[0, k]] == owner_ref[0]
                part = pl.ds((k + 1) * 128, 128)
                blocks[part, :] = jnp.where(keep, b_ref[part, :].astype(F32), 0.0).astype(BF16)

        target = coarse_rhs.astype(F32)
        ratio_now = HALF_WIDTH / CENTRE_VALUE
        direction = target / CENTRE_VALUE
        coarse = direction
        for step in range(CHEB):
            ratio_next = 1.0 / (2.0 * CENTRE_VALUE / HALF_WIDTH - ratio_now)
            turn = CHEB * it + step
            line_finish(turn)
            if step == 0:
                misfit = target - apply_coarse(turn, coarse_rhs) / CENTRE_VALUE
            else:
                misfit = target - apply_coarse(turn, coarse.astype(BF16))
            direction = (
                ratio_next * ratio_now * direction + 2.0 * ratio_next / HALF_WIDTH * misfit
            )
            coarse = coarse + direction
            ratio_now = ratio_next
            if step < CHEB - 1:
                line_start(turn + 1, coarse.astype(BF16))
        coarse = coarse.astype(BF16)

        def correct(j):
            update = smooth[:, cols(j)] + jnp.dot(
                coarse, z_ref[:, cols(j)], preferred_element_type=F32
            )
            smooth[:, cols(j)] = update
            scaled = row(0, j) * update
            wpad[:, pcols(padded(j))] = scaled
            if it == 0:
                sol_ref[:, cols(j)] = update
            else:
                sol_ref[:, cols(j)] = sol_ref[:, cols(j)] + update
            return scaled

        sides = (a % 2, 1 - a % 2)
        for turn, side in enumerate(sides):

            def correct_layer(y):
                scaled = correct(side * ((cx - 1) * cy) + y)
                xsend[it, side, :, cols(y)] = scaled.astype(BF16)

            each(0, cy, correct_layer)
            face_start(it, 0, side)
            if turn == 0:
                far_start(it)
        each(cy, (cx - 2) * cy, correct)
        far_forward(it)
        for side, y in enumerate((0, cy - 1)):
            for x in range(cx):
                ysend[it, side, :, pl.ds(x * cz, cz)] = wpad[
                    :, pl.ds(((x + 1) * pad_y + y + 1) * cz, cz)
                ].astype(BF16)
            face_start(it, 1, side)

        def gather(j, carry):
            low, high = carry
            first = wpad[:, pl.ds(pl.multiple_of(padded(j), 128), 128)]
            last = wpad[:, pl.ds(pl.multiple_of(padded(j) + cz - 128, 128), 128)]
            low = jnp.where(narrow == j, pltpu.roll(first, j, 1), low)
            high = jnp.where(narrow == j, pltpu.roll(last, j + 1, 1), high)
            return low, high

        empty = jnp.zeros((rows, 128), F32)
        low, high = lax.fori_loop(0, cx * cy, gather, (empty, empty))
        zsend[it, 0] = low.astype(BF16)
        zsend[it, 1] = high.astype(BF16)
        face_start(it, 2, 0)
        face_start(it, 2, 1)

        def apply_inside(j):
            res_ref[:, cols(j)] = (
                field[:, cols(j)]
                - row(1, j) * smooth[:, cols(j)]
                + row(0, j) * beside(padded(j))
            )

        each(0, cx * cy, apply_inside)

        face_wait(it, 2, 0)
        face_wait(it, 2, 1)
        zlow, zhigh = zrecv[it, 0].astype(F32), zrecv[it, 1].astype(F32)

        def add_z(j):
            first = pl.ds(pl.multiple_of(j * cz, 128), 128)
            last = pl.ds(pl.multiple_of(j * cz + cz - 128, 128), 128)
            scale = coef[0, pl.ds(j, 1), :]
            res_ref[:, first] = res_ref[:, first] + jnp.where(
                narrow == 0, scale[:, :128] * pltpu.roll(zlow, (128 - j) % 128, 1), 0.0
            )
            res_ref[:, last] = res_ref[:, last] + jnp.where(
                narrow == 127, scale[:, cz - 128 :] * pltpu.roll(zhigh, 127 - j, 1), 0.0
            )

        each(0, cx * cy, add_z)
        for side, y in enumerate((0, cy - 1)):
            face_wait(it, 1, side)
            for x in range(cx):
                j = x * cy + y
                part = pl.ds(j * cz, cz)
                res_ref[:, part] = res_ref[:, part] + coef[0, pl.ds(j, 1), :] * yrecv[
                    it, side, :, pl.ds(x * cz, cz)
                ].astype(F32)
        for turn, side in enumerate((1 - a % 2, a % 2)):
            if turn == 1 and it < ITERS - 1:
                coarse_rhs = restrict(False)
            face_wait(it, 0, side)
            if turn == 1:
                far_wait(it)
            x = side * (cx - 1)
            terms = []
            for y in range(cy):
                j = x * cy + y
                term = row(0, j) * xrecv[it, side, :, pl.ds(y * cz, cz)].astype(F32)
                res_ref[:, cols(j)] = res_ref[:, cols(j)] + term
                terms.append(term.astype(BF16))
            if turn == 1 and it < ITERS - 1:
                coarse_rhs = coarse_rhs + restrict_layer(jnp.concatenate(terms, axis=1), x)

    for it in range(ITERS):
        far_drain(it)
        for step in range(CHEB):
            line_drain(CHEB * it + step)
        for which in range(3):
            face_drain(it, which)
    others = owners.at[pl.ds(0, n_gz - 1)]
    pltpu.make_async_copy(others, others, owner_send_sem).wait()


def emit(sol_ref, res_ref, sol_out, res_out, sem):
    rows, cx, cy, cz = sol_out.shape
    copies = []
    for which, (source, target) in enumerate(((sol_ref, sol_out), (res_ref, res_out))):
        for x in range(cx):
            for y in range(cy):
                copies.append(
                    pltpu.make_async_copy(
                        source.at[:, pl.ds((x * cy + y) * cz, cz)],
                        target.at[:, x, y, :],
                        sem.at[which, x, y],
                    )
                )
    for copy in copies:
        copy.start()
    for copy in copies:
        copy.wait()


def local(sizes, right_side, stiffness, reaction, deflation, coarse_blocks, row_owner, neighbours):
    n_gx, n_gy, n_gz = sizes
    rows, cx, cy, cz = right_side.shape
    cells = cx * cy * cz
    vectors = deflation.shape[0]
    vmem = pl.BlockSpec(memory_space=pltpu.VMEM)
    smem = pl.BlockSpec(memory_space=pltpu.SMEM)
    hbm = pl.BlockSpec(memory_space=pl.ANY)
    turns = ITERS * CHEB
    flat = jax.ShapeDtypeStruct((rows, cells), F32)
    solution, residual = pl.pallas_call(
        functools.partial(kernel, (n_gx, n_gy, n_gz, cx, cy, cz)),
        out_shape=(flat, flat),
        in_specs=[hbm] * 3 + [vmem] * 2 + [smem] * 2,
        out_specs=(vmem, vmem),
        scratch_shapes=[
            pltpu.VMEM((2, cx * cy, cz), F32),
            pltpu.VMEM((4, cx * cy, cz), F32),
            pltpu.VMEM((rows, (cx + 2) * (cy + 2) * cz), F32),
            pltpu.VMEM((rows, cells), F32),
            pltpu.VMEM((7 * vectors, vectors), BF16),
            pltpu.VMEM((n_gz, 1, 128), jnp.int32),
            *[pltpu.VMEM((n_gz, rows, vectors), BF16)] * turns,
            pltpu.VMEM((ITERS, 2, rows, cy * cz), BF16),
            pltpu.VMEM((ITERS, 2, rows, cy * cz), BF16),
            pltpu.VMEM((ITERS, 2, rows, cx * cz), BF16),
            pltpu.VMEM((ITERS, 2, rows, cx * cz), BF16),
            pltpu.VMEM((ITERS, 2, rows, 128), BF16),
            pltpu.VMEM((ITERS, 2, rows, 128), BF16),
            pltpu.SemaphoreType.DMA,
            pltpu.SemaphoreType.DMA,
            pltpu.SemaphoreType.DMA((turns, n_gz)),
            pltpu.SemaphoreType.DMA((turns, n_gz)),
            pltpu.SemaphoreType.DMA((ITERS, 3, 2)),
            pltpu.SemaphoreType.DMA((ITERS, 3, 2)),
            pltpu.SemaphoreType.DMA((cx, cy)),
            pltpu.SemaphoreType.DMA((2, cx)),
            pltpu.VMEM((ITERS, rows, max(SHARES)), BF16),
            pltpu.SemaphoreType.DMA((ITERS, 2, len(SHARES))),
            pltpu.SemaphoreType.DMA((ITERS, 2, len(SHARES))),
        ],
        compiler_params=pltpu.CompilerParams(
            collective_id=0, has_side_effects=True, vmem_limit_bytes=28 * 1024 * 1024
        ),
        name="schwarz",
    )(
        right_side,
        stiffness,
        reaction,
        deflation.reshape(vectors, cells),
        coarse_blocks.reshape(7 * vectors, vectors),
        row_owner,
        neighbours,
    )
    whole = jax.ShapeDtypeStruct(right_side.shape, F32)
    return pl.pallas_call(
        emit,
        out_shape=(whole, whole),
        in_specs=[vmem, vmem],
        out_specs=(hbm, hbm),
        scratch_shapes=[pltpu.SemaphoreType.DMA((2, cx, cy))],
        compiler_params=pltpu.CompilerParams(vmem_limit_bytes=4 * 1024 * 1024),
        name="emit",
    )(solution, residual)


def solution(mesh):
    sizes = tuple(mesh.shape[name] for name in ("gx", "gy", "gz"))
    return jax.shard_map(
        functools.partial(local, sizes),
        mesh=mesh,
        in_specs=(
            P(None, "gx", "gy", "gz"),
            P("gx", "gy", "gz"),
            P("gx", "gy", "gz"),
            P(None, "gx", "gy", "gz"),
            P(("gx", "gy", "gz"), None, None, None),
            P(("gx", "gy", "gz")),
            P(("gx", "gy", "gz"), None),
        ),
        out_specs=(P(None, "gx", "gy", "gz"), P(None, "gx", "gy", "gz")),
        check_vma=False,
    )
```

```python
import functools

import jax
import jax.numpy as jnp
from jax import lax
from jax.experimental import pallas as pl
from jax.experimental.pallas import tpu as pltpu
from jax.sharding import PartitionSpec as P

ITERS = 2
CHEB = 2

RELAX_WEIGHT = 0.8
CENTRE_VALUE = 2.0
HALF_WIDTH = 1.0

SHARES = (384, 128, 128)

MESH = pl.DeviceIdType.MESH
F32 = jnp.float32
BF16 = jnp.bfloat16


def flip(place, bits):
    bit = 1
    while bit <= bits:
        if bits & bit:
            place = place + bit - 2 * bit * ((place // bit) % 2)
        bit *= 2
    return place


def kernel(
    sizes,
    r_ref,
    s_ref,
    react_ref,
    z_ref,
    b_ref,
    owner_ref,
    near_ref,
    sol_ref,
    res_ref,
    cells_in,
    coef,
    wpad,
    smooth,
    blocks,
    owners,
    line0,
    line1,
    line2,
    line3,
    xsend,
    xrecv,
    ysend,
    yrecv,
    zsend,
    zrecv,
    owner_send_sem,
    owner_recv_sem,
    line_send_sem,
    line_recv_sem,
    face_send_sem,
    face_recv_sem,
    field_sem,
    cells_sem,
    around,
    around_send_sem,
    around_recv_sem,
):
    n_gx, n_gy, n_gz, cx, cy, cz = sizes
    rows = res_ref.shape[0]
    n_chips = n_gz // 2
    pad_y = cy + 2
    a, b, g = lax.axis_index("gx"), lax.axis_index("gy"), lax.axis_index("gz")
    chip, core = g // 2, g % 2
    partner = chip * 2 + 1 - core
    line = (line0, line1, line2, line3)

    def at_line(place):
        return {"gz": place}

    half = n_gx // 2
    low_far, high_far = half - 1, half
    apart = (a - low_far) * (a - high_far)
    is_far = apart == 0
    ways, start = [], cy * cz
    for via, share in zip([0, *range(half - 2, 0, -1)], SHARES):
        start -= share
        ways.append((via, pl.ds(start, share), share))
    straight = pl.ds(0, start)

    def cells_copy(which, x):
        source = (s_ref, react_ref)[which]
        return pltpu.make_async_copy(
            source.at[x], cells_in.at[which, pl.ds(x * cy, cy), :], cells_sem.at[which, x]
        )

    def field_copy(x, y):
        return pltpu.make_async_copy(
            r_ref.at[:, x, y, :],
            res_ref.at[:, pl.ds((x * cy + y) * cz, cz)],
            field_sem.at[x, y],
        )

    barrier = pltpu.get_barrier_semaphore()
    @pl.when(is_far)
    def _():
        for other in [*range(low_far), *range(high_far + 1, n_gx)]:
            pl.semaphore_signal(
                barrier, inc=1, device_id={"gx": other}, device_id_type=MESH
            )

    @pl.when(apart > 0)
    def _():
        for other in (low_far, high_far):
            pl.semaphore_signal(
                barrier, inc=1, device_id={"gx": other}, device_id_type=MESH
            )

    for step in range(1, n_gz):
        pl.semaphore_signal(
            barrier, inc=1, device_id=at_line((g + step) % n_gz), device_id_type=MESH
        )
    places = (("gx", a, n_gx), ("gy", b, n_gy))
    for name, place, count in places:

        @pl.when(place > 0)
        def _():
            pl.semaphore_signal(
                barrier, inc=1, device_id={name: place - 1}, device_id_type=MESH
            )

        @pl.when(place < count - 1)
        def _():
            pl.semaphore_signal(
                barrier, inc=1, device_id={name: place + 1}, device_id_type=MESH
            )

    for x in range(cx):
        for y in range(cy):
            field_copy(x, y).start()
    for x in range(cx):
        for which in range(2):
            cells_copy(which, x).start()

    def coefficients():
        for x in range(cx):
            for which in range(2):
                cells_copy(which, x).wait()
        stiff = cells_in[0]
        diagonal = 6.0 * stiff * stiff + cells_in[1]
        relax = RELAX_WEIGHT / diagonal
        coef[0] = stiff
        coef[1] = diagonal
        coef[2] = (2.0 - RELAX_WEIGHT) * relax
        coef[3] = stiff * relax

    lane = lax.broadcasted_iota(jnp.int32, (rows, cz), 1)
    narrow = lax.broadcasted_iota(jnp.int32, (rows, 128), 1)

    def cols(j):
        return pl.ds(pl.multiple_of(j * cz, cz), cz)

    def padded(j):
        x, y = j // cy, j % cy
        return ((x + 1) * pad_y + y + 1) * cz

    def pcols(offset):
        return pl.ds(pl.multiple_of(offset, cz), cz)

    def row(which, j):
        return coef[which, pl.ds(j, 1), :]

    def beside(offset):
        centre = wpad[:, pcols(offset)]
        total = wpad[:, pcols(offset + pad_y * cz)] + wpad[:, pcols(offset - pad_y * cz)]
        total = total + wpad[:, pcols(offset + cz)] + wpad[:, pcols(offset - cz)]
        total = total + jnp.where(lane == cz - 1, 0.0, pltpu.roll(centre, cz - 1, 1))
        return total + jnp.where(lane == 0, 0.0, pltpu.roll(centre, 1, 1))

    def each(first, count, body):
        def step(i, carry):
            body(first + i)
            return carry

        lax.fori_loop(0, count, step, 0)

    def clear():
        zero_row = jnp.zeros((rows, pad_y * cz), F32)
        wpad[:, pl.ds(0, pad_y * cz)] = zero_row
        wpad[:, pl.ds((cx + 1) * pad_y * cz, pad_y * cz)] = zero_row
        for x in range(cx):
            wpad[:, pl.ds((x + 1) * pad_y * cz, cz)] = jnp.zeros((rows, cz), F32)
            wpad[:, pl.ds(((x + 2) * pad_y - 1) * cz, cz)] = jnp.zeros((rows, cz), F32)

        faces = (("gx", a, n_gx, xrecv), ("gy", b, n_gy, yrecv), ("gz", g, n_gz, zrecv))
        for it in range(ITERS):
            for name, place, count, recv in faces:

                @pl.when(place == 0)
                def _():
                    recv[it, 0] = jnp.zeros(recv.shape[2:], recv.dtype)

                @pl.when(place == count - 1)
                def _():
                    recv[it, 1] = jnp.zeros(recv.shape[2:], recv.dtype)

    width = cy * cz

    def restrict_layer(values, x):
        return lax.dot_general(
            values.astype(BF16),
            z_ref[:, pl.ds(pl.multiple_of(x * width, width), width)],
            (((1,), (1,)), ((), ())),
            preferred_element_type=F32,
        )

    def restrict(first):
        total = jnp.zeros((rows, z_ref.shape[0]), F32)
        for x in range(cx):
            if first:
                for y in range(cy):
                    field_copy(x, y).wait()
            total = total + restrict_layer(res_ref[:, pl.ds(x * width, width)], x)
        return total

    def line_copy(turn, slot, sem, target):
        return pltpu.make_async_remote_copy(
            src_ref=line[turn].at[slot],
            dst_ref=line[turn].at[slot],
            send_sem=line_send_sem.at[turn, sem],
            recv_sem=line_recv_sem.at[turn, slot],
            device_id=at_line(target),
            device_id_type=MESH,
        )

    def line_start(turn, value):
        line[turn][g] = value
        for bits in range(n_chips - 1, 0, -1):
            line_copy(turn, g, bits, flip(chip, bits) * 2 + core).start()
        line_copy(turn, g, 0, partner).start()

    def line_finish(turn):
        for bits in range(1, n_chips):
            source = flip(chip, bits) * 2 + core
            line_copy(turn, source, 0, partner).wait_recv()
            line_copy(turn, source, n_chips + bits, partner).start()
        line_copy(turn, partner, 0, partner).wait_recv()
        for bits in range(1, n_chips):
            source = flip(chip, bits) * 2 + 1 - core
            line_copy(turn, source, 0, partner).wait_recv()

    def line_drain(turn):
        for sem in range(n_chips):
            line_copy(turn, g, sem, partner).wait_send()
        for bits in range(1, n_chips):
            line_copy(turn, g, n_chips + bits, partner).wait_send()

    def face_copy(it, axis, side, send, recv, name, target):
        return pltpu.make_async_remote_copy(
            src_ref=send.at[it, side],
            dst_ref=recv.at[it, 1 - side],
            send_sem=face_send_sem.at[it, axis, side],
            recv_sem=face_recv_sem.at[it, axis, 1 - side],
            device_id={name: target},
            device_id_type=MESH,
        )

    exchange = (
        (0, "gx", a, n_gx, xsend, xrecv),
        (1, "gy", b, n_gy, ysend, yrecv),
        (2, "gz", g, n_gz, zsend, zrecv),
    )

    def touches(which, place, side, other, count):
        inside = (other >= 0) & (other < count)
        if which == 0:
            inside = inside & (place + other != low_far + high_far)
        return inside

    def face_start(it, which, side):
        axis, name, place, count, send, recv = exchange[which]
        target = place - 1 + 2 * side

        @pl.when(touches(which, place, side, target, count))
        def _():
            face_copy(it, axis, side, send, recv, name, target).start()

    def face_wait(it, which, side):
        axis, name, place, count, send, recv = exchange[which]
        source = place - 1 + 2 * side

        @pl.when(touches(which, place, side, source, count))
        def _():
            face_copy(it, axis, 1 - side, send, recv, name, source).wait_recv()

    far_side = a % 2
    far_place = low_far + high_far - a

    def straight_copy(it, slot):
        return pltpu.make_async_remote_copy(
            src_ref=xsend.at[it, far_side, :, straight],
            dst_ref=xrecv.at[it, slot, :, straight],
            send_sem=face_send_sem.at[it, 0, far_side],
            recv_sem=face_recv_sem.at[it, 0, slot],
            device_id={"gx": far_place},
            device_id_type=MESH,
        )

    def out_copy(it, way):
        via, part, share = ways[way]
        return pltpu.make_async_remote_copy(
            src_ref=xsend.at[it, far_side, :, part],
            dst_ref=around.at[it, :, pl.ds(0, share)],
            send_sem=around_send_sem.at[it, 0, way],
            recv_sem=around_recv_sem.at[it, 0, way],
            device_id={"gx": via + (1 - far_side) * (n_gx - 1 - 2 * via)},
            device_id_type=MESH,
        )

    def on_copy(it, way, slot, target):
        via, part, share = ways[way]
        return pltpu.make_async_remote_copy(
            src_ref=around.at[it, :, pl.ds(0, share)],
            dst_ref=xrecv.at[it, slot, :, part],
            send_sem=around_send_sem.at[it, 1, way],
            recv_sem=around_recv_sem.at[it, 1, way],
            device_id={"gx": target},
            device_id_type=MESH,
        )

    def far_start(it):
        @pl.when(is_far)
        def _():
            for way in range(len(ways)):
                out_copy(it, way).start()
            straight_copy(it, 1 - far_side).start()

    def each_via(action):
        for way, (via, part, share) in enumerate(ways):

            @pl.when((a - via) * (a - (n_gx - 1 - via)) == 0)
            def _():
                action(way)

    def far_forward(it):
        def forward(way):
            out_copy(it, way).wait_recv()
            on_copy(it, way, a // half, high_far - a // half).start()

        each_via(forward)

    def far_wait(it):
        @pl.when(is_far)
        def _():
            straight_copy(it, far_side).wait_recv()
            for way in range(len(ways)):
                on_copy(it, way, far_side, far_place).wait_recv()

    def far_drain(it):
        @pl.when(is_far)
        def _():
            straight_copy(it, 1 - far_side).wait_send()
            for way in range(len(ways)):
                out_copy(it, way).wait_send()

        each_via(lambda way: on_copy(it, way, a // half, high_far - a // half).wait_send())

    def face_drain(it, which):
        axis, name, place, count, send, recv = exchange[which]
        for side in range(2):
            target = place - 1 + 2 * side

            @pl.when(touches(which, place, side, target, count))
            def _():
                face_copy(it, axis, side, send, recv, name, target).wait_send()

    def relaxed(field):
        def scale(j):
            wpad[:, pcols(padded(j))] = row(3, j) * field[:, cols(j)]

        def combine(j):
            smooth[:, cols(j)] = row(2, j) * field[:, cols(j)] + row(3, j) * beside(padded(j))

        each(0, cx * cy, scale)
        each(0, cx * cy, combine)

    def apply_coarse(turn, value):
        picked = [value] + [line[turn][near_ref[0, k]] for k in range(6)]
        return jnp.dot(
            jnp.concatenate(picked, axis=1), blocks[...], preferred_element_type=F32
        )

    def owner_copy(target):
        return pltpu.make_async_remote_copy(
            src_ref=owners.at[g],
            dst_ref=owners.at[g],
            send_sem=owner_send_sem,
            recv_sem=owner_recv_sem,
            device_id=at_line(target),
            device_id_type=MESH,
        )

    owners[g] = jnp.full((1, 128), owner_ref[0], jnp.int32)
    for it in range(ITERS):
        field = res_ref
        if it == 0:
            coarse_rhs = restrict(True)
        coarse_rhs = coarse_rhs.astype(BF16)
        if it == 0:
            peers = n_gz - 1
            for name, place, count in places:
                for way in (place, count - 1 - place):
                    peers = peers + (way + count - 1) // count
            most = n_gx * n_gx
            peers = peers + 2 + (n_gx - 4) * (1 - (apart + most - 1) // most)
            pl.semaphore_wait(barrier, peers)
            for step in range(1, n_gz):
                owner_copy((g + step) % n_gz).start()
        line_start(CHEB * it, coarse_rhs)
        if it == 0:
            coefficients()
            clear()
        relaxed(field)
        if it == 0:
            others = owners.at[pl.ds(0, n_gz - 1)]
            pltpu.make_async_copy(others, others, owner_recv_sem).wait()
            blocks[pl.ds(0, 128), :] = b_ref[pl.ds(0, 128), :]
            for k in range(6):
                keep = owners[near_ref[0, k]] == owner_ref[0]
                part = pl.ds((k + 1) * 128, 128)
                blocks[part, :] = jnp.where(keep, b_ref[part, :].astype(F32), 0.0).astype(BF16)

        target = coarse_rhs.astype(F32)
        ratio_now = HALF_WIDTH / CENTRE_VALUE
        direction = target / CENTRE_VALUE
        coarse = direction
        for step in range(CHEB):
            ratio_next = 1.0 / (2.0 * CENTRE_VALUE / HALF_WIDTH - ratio_now)
            turn = CHEB * it + step
            line_finish(turn)
            if step == 0:
                misfit = target - apply_coarse(turn, coarse_rhs) / CENTRE_VALUE
            else:
                misfit = target - apply_coarse(turn, coarse.astype(BF16))
            direction = (
                ratio_next * ratio_now * direction + 2.0 * ratio_next / HALF_WIDTH * misfit
            )
            coarse = coarse + direction
            ratio_now = ratio_next
            if step < CHEB - 1:
                line_start(turn + 1, coarse.astype(BF16))
        coarse = coarse.astype(BF16)

        def correct(j):
            update = smooth[:, cols(j)] + jnp.dot(
                coarse, z_ref[:, cols(j)], preferred_element_type=F32
            )
            smooth[:, cols(j)] = update
            scaled = row(0, j) * update
            wpad[:, pcols(padded(j))] = scaled
            if it == 0:
                sol_ref[:, cols(j)] = update
            else:
                sol_ref[:, cols(j)] = sol_ref[:, cols(j)] + update
            return scaled

        sides = (a % 2, 1 - a % 2)
        for turn, side in enumerate(sides):

            def correct_layer(y):
                scaled = correct(side * ((cx - 1) * cy) + y)
                xsend[it, side, :, cols(y)] = scaled.astype(BF16)

            each(0, cy, correct_layer)
            face_start(it, 0, side)
            if turn == 0:
                far_start(it)
        each(cy, (cx - 2) * cy, correct)
        far_forward(it)
        for side, y in enumerate((0, cy - 1)):
            for x in range(cx):
                ysend[it, side, :, pl.ds(x * cz, cz)] = wpad[
                    :, pl.ds(((x + 1) * pad_y + y + 1) * cz, cz)
                ].astype(BF16)
            face_start(it, 1, side)

        def gather(j, carry):
            low, high = carry
            first = wpad[:, pl.ds(pl.multiple_of(padded(j), 128), 128)]
            last = wpad[:, pl.ds(pl.multiple_of(padded(j) + cz - 128, 128), 128)]
            low = jnp.where(narrow == j, pltpu.roll(first, j, 1), low)
            high = jnp.where(narrow == j, pltpu.roll(last, j + 1, 1), high)
            return low, high

        empty = jnp.zeros((rows, 128), F32)
        low, high = lax.fori_loop(0, cx * cy, gather, (empty, empty))
        zsend[it, 0] = low.astype(BF16)
        zsend[it, 1] = high.astype(BF16)
        face_start(it, 2, 0)
        face_start(it, 2, 1)

        def apply_inside(j):
            res_ref[:, cols(j)] = (
                field[:, cols(j)]
                - row(1, j) * smooth[:, cols(j)]
                + row(0, j) * beside(padded(j))
            )

        each(0, cx * cy, apply_inside)

        face_wait(it, 2, 0)
        face_wait(it, 2, 1)
        zlow, zhigh = zrecv[it, 0].astype(F32), zrecv[it, 1].astype(F32)

        def add_z(j):
            first = pl.ds(pl.multiple_of(j * cz, 128), 128)
            last = pl.ds(pl.multiple_of(j * cz + cz - 128, 128), 128)
            scale = coef[0, pl.ds(j, 1), :]
            res_ref[:, first] = res_ref[:, first] + jnp.where(
                narrow == 0, scale[:, :128] * pltpu.roll(zlow, (128 - j) % 128, 1), 0.0
            )
            res_ref[:, last] = res_ref[:, last] + jnp.where(
                narrow == 127, scale[:, cz - 128 :] * pltpu.roll(zhigh, 127 - j, 1), 0.0
            )

        each(0, cx * cy, add_z)
        for side, y in enumerate((0, cy - 1)):
            face_wait(it, 1, side)
            for x in range(cx):
                j = x * cy + y
                part = pl.ds(j * cz, cz)
                res_ref[:, part] = res_ref[:, part] + coef[0, pl.ds(j, 1), :] * yrecv[
                    it, side, :, pl.ds(x * cz, cz)
                ].astype(F32)
        for turn, side in enumerate((1 - a % 2, a % 2)):
            if turn == 1 and it < ITERS - 1:
                coarse_rhs = restrict(False)
            face_wait(it, 0, side)
            if turn == 1:
                far_wait(it)
            x = side * (cx - 1)
            terms = []
            for y in range(cy):
                j = x * cy + y
                term = row(0, j) * xrecv[it, side, :, pl.ds(y * cz, cz)].astype(F32)
                res_ref[:, cols(j)] = res_ref[:, cols(j)] + term
                terms.append(term.astype(BF16))
            if turn == 1 and it < ITERS - 1:
                coarse_rhs = coarse_rhs + restrict_layer(jnp.concatenate(terms, axis=1), x)

    for it in range(ITERS):
        far_drain(it)
        for step in range(CHEB):
            line_drain(CHEB * it + step)
        for which in range(3):
            face_drain(it, which)
    others = owners.at[pl.ds(0, n_gz - 1)]
    pltpu.make_async_copy(others, others, owner_send_sem).wait()


def emit(sol_ref, res_ref, sol_out, res_out, sem):
    rows, cx, cy, cz = sol_out.shape
    copies = []
    for which, (source, target) in enumerate(((sol_ref, sol_out), (res_ref, res_out))):
        for x in range(cx):
            for y in range(cy):
                copies.append(
                    pltpu.make_async_copy(
                        source.at[:, pl.ds((x * cy + y) * cz, cz)],
                        target.at[:, x, y, :],
                        sem.at[which, x, y],
                    )
                )
    for copy in copies:
        copy.start()
    for copy in copies:
        copy.wait()


def local(sizes, right_side, stiffness, reaction, deflation, coarse_blocks, row_owner, neighbours):
    n_gx, n_gy, n_gz = sizes
    rows, cx, cy, cz = right_side.shape
    cells = cx * cy * cz
    vectors = deflation.shape[0]
    vmem = pl.BlockSpec(memory_space=pltpu.VMEM)
    smem = pl.BlockSpec(memory_space=pltpu.SMEM)
    hbm = pl.BlockSpec(memory_space=pl.ANY)
    turns = ITERS * CHEB
    flat = jax.ShapeDtypeStruct((rows, cells), F32)
    solution, residual = pl.pallas_call(
        functools.partial(kernel, (n_gx, n_gy, n_gz, cx, cy, cz)),
        out_shape=(flat, flat),
        in_specs=[hbm] * 3 + [vmem] * 2 + [smem] * 2,
        out_specs=(vmem, vmem),
        scratch_shapes=[
            pltpu.VMEM((2, cx * cy, cz), F32),
            pltpu.VMEM((4, cx * cy, cz), F32),
            pltpu.VMEM((rows, (cx + 2) * (cy + 2) * cz), F32),
            pltpu.VMEM((rows, cells), F32),
            pltpu.VMEM((7 * vectors, vectors), BF16),
            pltpu.VMEM((n_gz, 1, 128), jnp.int32),
            *[pltpu.VMEM((n_gz, rows, vectors), BF16)] * turns,
            pltpu.VMEM((ITERS, 2, rows, cy * cz), BF16),
            pltpu.VMEM((ITERS, 2, rows, cy * cz), BF16),
            pltpu.VMEM((ITERS, 2, rows, cx * cz), BF16),
            pltpu.VMEM((ITERS, 2, rows, cx * cz), BF16),
            pltpu.VMEM((ITERS, 2, rows, 128), BF16),
            pltpu.VMEM((ITERS, 2, rows, 128), BF16),
            pltpu.SemaphoreType.DMA,
            pltpu.SemaphoreType.DMA,
            pltpu.SemaphoreType.DMA((turns, n_gz)),
            pltpu.SemaphoreType.DMA((turns, n_gz)),
            pltpu.SemaphoreType.DMA((ITERS, 3, 2)),
            pltpu.SemaphoreType.DMA((ITERS, 3, 2)),
            pltpu.SemaphoreType.DMA((cx, cy)),
            pltpu.SemaphoreType.DMA((2, cx)),
            pltpu.VMEM((ITERS, rows, max(SHARES)), BF16),
            pltpu.SemaphoreType.DMA((ITERS, 2, len(SHARES))),
            pltpu.SemaphoreType.DMA((ITERS, 2, len(SHARES))),
        ],
        compiler_params=pltpu.CompilerParams(
            collective_id=0, has_side_effects=True, vmem_limit_bytes=28 * 1024 * 1024
        ),
        name="schwarz",
    )(
        right_side,
        stiffness,
        reaction,
        deflation.reshape(vectors, cells),
        coarse_blocks.reshape(7 * vectors, vectors),
        row_owner,
        neighbours,
    )
    whole = jax.ShapeDtypeStruct(right_side.shape, F32)
    return pl.pallas_call(
        emit,
        out_shape=(whole, whole),
        in_specs=[vmem, vmem],
        out_specs=(hbm, hbm),
        scratch_shapes=[pltpu.SemaphoreType.DMA((2, cx, cy))],
        compiler_params=pltpu.CompilerParams(vmem_limit_bytes=4 * 1024 * 1024),
        name="emit",
    )(solution, residual)


def solution(mesh):
    sizes = tuple(mesh.shape[name] for name in ("gx", "gy", "gz"))
    return jax.shard_map(
        functools.partial(local, sizes),
        mesh=mesh,
        in_specs=(
            P(None, "gx", "gy", "gz"),
            P("gx", "gy", "gz"),
            P("gx", "gy", "gz"),
            P(None, "gx", "gy", "gz"),
            P(("gx", "gy", "gz"), None, None, None),
            P(("gx", "gy", "gz")),
            P(("gx", "gy", "gz"), None),
        ),
        out_specs=(P(None, "gx", "gy", "gz"), P(None, "gx", "gy", "gz")),
        check_vma=False,
    )
```

```python
import functools

import jax
import jax.numpy as jnp
from jax import lax
from jax.experimental import pallas as pl
from jax.experimental.pallas import tpu as pltpu
from jax.sharding import PartitionSpec as P

ITERS = 2
CHEB = 2

RELAX_WEIGHT = 0.8
CENTRE_VALUE = 2.0
HALF_WIDTH = 1.0

SHARES = (384, 128, 128)

MESH = pl.DeviceIdType.MESH
F32 = jnp.float32
BF16 = jnp.bfloat16


def flip(place, bits):
    bit = 1
    while bit <= bits:
        if bits & bit:
            place = place + bit - 2 * bit * ((place // bit) % 2)
        bit *= 2
    return place


def kernel(
    sizes,
    r_ref,
    s_ref,
    react_ref,
    z_ref,
    b_ref,
    owner_ref,
    near_ref,
    sol_ref,
    res_ref,
    cells_in,
    coef,
    wpad,
    smooth,
    blocks,
    owners,
    line0,
    line1,
    line2,
    line3,
    xsend,
    xrecv,
    ysend,
    yrecv,
    zsend,
    zrecv,
    owner_send_sem,
    owner_recv_sem,
    line_send_sem,
    line_recv_sem,
    face_send_sem,
    face_recv_sem,
    field_sem,
    cells_sem,
    around,
    around_send_sem,
    around_recv_sem,
):
    n_gx, n_gy, n_gz, cx, cy, cz = sizes
    rows = res_ref.shape[0]
    n_chips = n_gz // 2
    pad_y = cy + 2
    a, b, g = lax.axis_index("gx"), lax.axis_index("gy"), lax.axis_index("gz")
    chip, core = g // 2, g % 2
    partner = chip * 2 + 1 - core
    line = (line0, line1, line2, line3)

    def at_line(place):
        return {"gz": place}

    half = n_gx // 2
    low_far, high_far = half - 1, half
    apart = (a - low_far) * (a - high_far)
    is_far = apart == 0
    ways, start = [], cy * cz
    for via, share in zip([0, *range(half - 2, 0, -1)], SHARES):
        start -= share
        ways.append((via, pl.ds(start, share), share))
    straight = pl.ds(0, start)

    def cells_copy(which, x):
        source = (s_ref, react_ref)[which]
        return pltpu.make_async_copy(
            source.at[x], cells_in.at[which, pl.ds(x * cy, cy), :], cells_sem.at[which, x]
        )

    def field_copy(x, y):
        return pltpu.make_async_copy(
            r_ref.at[:, x, y, :],
            res_ref.at[:, pl.ds((x * cy + y) * cz, cz)],
            field_sem.at[x, y],
        )

    barrier = pltpu.get_barrier_semaphore()
    @pl.when(is_far)
    def _():
        for other in [*range(low_far), *range(high_far + 1, n_gx)]:
            pl.semaphore_signal(
                barrier, inc=1, device_id={"gx": other}, device_id_type=MESH
            )

    @pl.when(apart > 0)
    def _():
        for other in (low_far, high_far):
            pl.semaphore_signal(
                barrier, inc=1, device_id={"gx": other}, device_id_type=MESH
            )

    for step in range(1, n_gz):
        pl.semaphore_signal(
            barrier, inc=1, device_id=at_line((g + step) % n_gz), device_id_type=MESH
        )
    places = (("gx", a, n_gx), ("gy", b, n_gy))
    for name, place, count in places:

        @pl.when(place > 0)
        def _():
            pl.semaphore_signal(
                barrier, inc=1, device_id={name: place - 1}, device_id_type=MESH
            )

        @pl.when(place < count - 1)
        def _():
            pl.semaphore_signal(
                barrier, inc=1, device_id={name: place + 1}, device_id_type=MESH
            )

    for x in range(cx):
        for y in range(cy):
            field_copy(x, y).start()
    for x in range(cx):
        for which in range(2):
            cells_copy(which, x).start()

    def coefficients():
        for x in range(cx):
            for which in range(2):
                cells_copy(which, x).wait()
        stiff = cells_in[0]
        diagonal = 6.0 * stiff * stiff + cells_in[1]
        relax = RELAX_WEIGHT / diagonal
        coef[0] = stiff
        coef[1] = diagonal
        coef[2] = (2.0 - RELAX_WEIGHT) * relax
        coef[3] = stiff * relax

    lane = lax.broadcasted_iota(jnp.int32, (rows, cz), 1)
    narrow = lax.broadcasted_iota(jnp.int32, (rows, 128), 1)

    def cols(j):
        return pl.ds(pl.multiple_of(j * cz, cz), cz)

    def padded(j):
        x, y = j // cy, j % cy
        return ((x + 1) * pad_y + y + 1) * cz

    def pcols(offset):
        return pl.ds(pl.multiple_of(offset, cz), cz)

    def row(which, j):
        return coef[which, pl.ds(j, 1), :]

    def beside(offset):
        centre = wpad[:, pcols(offset)]
        total = wpad[:, pcols(offset + pad_y * cz)] + wpad[:, pcols(offset - pad_y * cz)]
        total = total + wpad[:, pcols(offset + cz)] + wpad[:, pcols(offset - cz)]
        total = total + jnp.where(lane == cz - 1, 0.0, pltpu.roll(centre, cz - 1, 1))
        return total + jnp.where(lane == 0, 0.0, pltpu.roll(centre, 1, 1))

    def each(first, count, body):
        def step(i, carry):
            body(first + i)
            return carry

        lax.fori_loop(0, count, step, 0)

    def clear():
        zero_row = jnp.zeros((rows, pad_y * cz), F32)
        wpad[:, pl.ds(0, pad_y * cz)] = zero_row
        wpad[:, pl.ds((cx + 1) * pad_y * cz, pad_y * cz)] = zero_row
        for x in range(cx):
            wpad[:, pl.ds((x + 1) * pad_y * cz, cz)] = jnp.zeros((rows, cz), F32)
            wpad[:, pl.ds(((x + 2) * pad_y - 1) * cz, cz)] = jnp.zeros((rows, cz), F32)

        faces = (("gx", a, n_gx, xrecv), ("gy", b, n_gy, yrecv), ("gz", g, n_gz, zrecv))
        for it in range(ITERS):
            for name, place, count, recv in faces:

                @pl.when(place == 0)
                def _():
                    recv[it, 0] = jnp.zeros(recv.shape[2:], recv.dtype)

                @pl.when(place == count - 1)
                def _():
                    recv[it, 1] = jnp.zeros(recv.shape[2:], recv.dtype)

    width = cy * cz

    def restrict_layer(values, x):
        return lax.dot_general(
            values.astype(BF16),
            z_ref[:, pl.ds(pl.multiple_of(x * width, width), width)],
            (((1,), (1,)), ((), ())),
            preferred_element_type=F32,
        )

    def restrict(first):
        total = jnp.zeros((rows, z_ref.shape[0]), F32)
        for x in range(cx):
            if first:
                for y in range(cy):
                    field_copy(x, y).wait()
            total = total + restrict_layer(res_ref[:, pl.ds(x * width, width)], x)
        return total

    def line_copy(turn, slot, sem, target):
        return pltpu.make_async_remote_copy(
            src_ref=line[turn].at[slot],
            dst_ref=line[turn].at[slot],
            send_sem=line_send_sem.at[turn, sem],
            recv_sem=line_recv_sem.at[turn, slot],
            device_id=at_line(target),
            device_id_type=MESH,
        )

    def line_start(turn, value):
        line[turn][g] = value
        for bits in range(n_chips - 1, 0, -1):
            line_copy(turn, g, bits, flip(chip, bits) * 2 + core).start()
        line_copy(turn, g, 0, partner).start()

    def line_finish(turn):
        for bits in range(1, n_chips):
            source = flip(chip, bits) * 2 + core
            line_copy(turn, source, 0, partner).wait_recv()
            line_copy(turn, source, n_chips + bits, partner).start()
        line_copy(turn, partner, 0, partner).wait_recv()
        for bits in range(1, n_chips):
            source = flip(chip, bits) * 2 + 1 - core
            line_copy(turn, source, 0, partner).wait_recv()

    def line_drain(turn):
        for sem in range(n_chips):
            line_copy(turn, g, sem, partner).wait_send()
        for bits in range(1, n_chips):
            line_copy(turn, g, n_chips + bits, partner).wait_send()

    def face_copy(it, axis, side, send, recv, name, target):
        return pltpu.make_async_remote_copy(
            src_ref=send.at[it, side],
            dst_ref=recv.at[it, 1 - side],
            send_sem=face_send_sem.at[it, axis, side],
            recv_sem=face_recv_sem.at[it, axis, 1 - side],
            device_id={name: target},
            device_id_type=MESH,
        )

    exchange = (
        (0, "gx", a, n_gx, xsend, xrecv),
        (1, "gy", b, n_gy, ysend, yrecv),
        (2, "gz", g, n_gz, zsend, zrecv),
    )

    def touches(which, place, side, other, count):
        inside = (other >= 0) & (other < count)
        if which == 0:
            inside = inside & (place + other != low_far + high_far)
        return inside

    def face_start(it, which, side):
        axis, name, place, count, send, recv = exchange[which]
        target = place - 1 + 2 * side

        @pl.when(touches(which, place, side, target, count))
        def _():
            face_copy(it, axis, side, send, recv, name, target).start()

    def face_wait(it, which, side):
        axis, name, place, count, send, recv = exchange[which]
        source = place - 1 + 2 * side

        @pl.when(touches(which, place, side, source, count))
        def _():
            face_copy(it, axis, 1 - side, send, recv, name, source).wait_recv()

    far_side = a % 2
    far_place = low_far + high_far - a

    def straight_copy(it, slot):
        return pltpu.make_async_remote_copy(
            src_ref=xsend.at[it, far_side, :, straight],
            dst_ref=xrecv.at[it, slot, :, straight],
            send_sem=face_send_sem.at[it, 0, far_side],
            recv_sem=face_recv_sem.at[it, 0, slot],
            device_id={"gx": far_place},
            device_id_type=MESH,
        )

    def out_copy(it, way):
        via, part, share = ways[way]
        return pltpu.make_async_remote_copy(
            src_ref=xsend.at[it, far_side, :, part],
            dst_ref=around.at[it, :, pl.ds(0, share)],
            send_sem=around_send_sem.at[it, 0, way],
            recv_sem=around_recv_sem.at[it, 0, way],
            device_id={"gx": via + (1 - far_side) * (n_gx - 1 - 2 * via)},
            device_id_type=MESH,
        )

    def on_copy(it, way, slot, target):
        via, part, share = ways[way]
        return pltpu.make_async_remote_copy(
            src_ref=around.at[it, :, pl.ds(0, share)],
            dst_ref=xrecv.at[it, slot, :, part],
            send_sem=around_send_sem.at[it, 1, way],
            recv_sem=around_recv_sem.at[it, 1, way],
            device_id={"gx": target},
            device_id_type=MESH,
        )

    def far_start(it):
        @pl.when(is_far)
        def _():
            for way in range(len(ways)):
                out_copy(it, way).start()
            straight_copy(it, 1 - far_side).start()

    def each_via(action):
        for way, (via, part, share) in enumerate(ways):

            @pl.when((a - via) * (a - (n_gx - 1 - via)) == 0)
            def _():
                action(way)

    def far_forward(it):
        def forward(way):
            out_copy(it, way).wait_recv()
            on_copy(it, way, a // half, high_far - a // half).start()

        each_via(forward)

    def far_wait(it):
        @pl.when(is_far)
        def _():
            straight_copy(it, far_side).wait_recv()
            for way in range(len(ways)):
                on_copy(it, way, far_side, far_place).wait_recv()

    def far_drain(it):
        @pl.when(is_far)
        def _():
            straight_copy(it, 1 - far_side).wait_send()
            for way in range(len(ways)):
                out_copy(it, way).wait_send()

        each_via(lambda way: on_copy(it, way, a // half, high_far - a // half).wait_send())

    def face_drain(it, which):
        axis, name, place, count, send, recv = exchange[which]
        for side in range(2):
            target = place - 1 + 2 * side

            @pl.when(touches(which, place, side, target, count))
            def _():
                face_copy(it, axis, side, send, recv, name, target).wait_send()

    def relaxed(field):
        def scale(j):
            wpad[:, pcols(padded(j))] = row(3, j) * field[:, cols(j)]

        def combine(j):
            smooth[:, cols(j)] = row(2, j) * field[:, cols(j)] + row(3, j) * beside(padded(j))

        each(0, cx * cy, scale)
        each(0, cx * cy, combine)

    def apply_coarse(turn, value):
        picked = [value] + [line[turn][near_ref[0, k]] for k in range(6)]
        return jnp.dot(
            jnp.concatenate(picked, axis=1), blocks[...], preferred_element_type=F32
        )

    def owner_copy(target):
        return pltpu.make_async_remote_copy(
            src_ref=owners.at[g],
            dst_ref=owners.at[g],
            send_sem=owner_send_sem,
            recv_sem=owner_recv_sem,
            device_id=at_line(target),
            device_id_type=MESH,
        )

    owners[g] = jnp.full((1, 128), owner_ref[0], jnp.int32)
    for it in range(ITERS):
        field = res_ref
        if it == 0:
            coarse_rhs = restrict(True)
        coarse_rhs = coarse_rhs.astype(BF16)
        if it == 0:
            peers = n_gz - 1
            for name, place, count in places:
                for way in (place, count - 1 - place):
                    peers = peers + (way + count - 1) // count
            most = n_gx * n_gx
            peers = peers + 2 + (n_gx - 4) * (1 - (apart + most - 1) // most)
            pl.semaphore_wait(barrier, peers)
        line_start(CHEB * it, coarse_rhs)
        if it == 0:
            for step in range(1, n_gz):
                owner_copy((g + step) % n_gz).start()
        if it == 0:
            coefficients()
            clear()
        relaxed(field)
        if it == 0:
            others = owners.at[pl.ds(0, n_gz - 1)]
            pltpu.make_async_copy(others, others, owner_recv_sem).wait()
            blocks[pl.ds(0, 128), :] = b_ref[pl.ds(0, 128), :]
            for k in range(6):
                keep = owners[near_ref[0, k]] == owner_ref[0]
                part = pl.ds((k + 1) * 128, 128)
                blocks[part, :] = jnp.where(keep, b_ref[part, :].astype(F32), 0.0).astype(BF16)

        target = coarse_rhs.astype(F32)
        ratio_now = HALF_WIDTH / CENTRE_VALUE
        direction = target / CENTRE_VALUE
        coarse = direction
        for step in range(CHEB):
            ratio_next = 1.0 / (2.0 * CENTRE_VALUE / HALF_WIDTH - ratio_now)
            turn = CHEB * it + step
            line_finish(turn)
            if step == 0:
                misfit = target - apply_coarse(turn, coarse_rhs) / CENTRE_VALUE
            else:
                misfit = target - apply_coarse(turn, coarse.astype(BF16))
            direction = (
                ratio_next * ratio_now * direction + 2.0 * ratio_next / HALF_WIDTH * misfit
            )
            coarse = coarse + direction
            ratio_now = ratio_next
            if step < CHEB - 1:
                line_start(turn + 1, coarse.astype(BF16))
        coarse = coarse.astype(BF16)

        def correct(j):
            update = smooth[:, cols(j)] + jnp.dot(
                coarse, z_ref[:, cols(j)], preferred_element_type=F32
            )
            smooth[:, cols(j)] = update
            scaled = row(0, j) * update
            wpad[:, pcols(padded(j))] = scaled
            if it == 0:
                sol_ref[:, cols(j)] = update
            else:
                sol_ref[:, cols(j)] = sol_ref[:, cols(j)] + update
            return scaled

        sides = (a % 2, 1 - a % 2)
        for turn, side in enumerate(sides):

            def correct_layer(y):
                scaled = correct(side * ((cx - 1) * cy) + y)
                xsend[it, side, :, cols(y)] = scaled.astype(BF16)

            for y in range(cy):
                correct_layer(y)
            face_start(it, 0, side)
            if turn == 0:
                far_start(it)
        each(cy, (cx - 2) * cy, correct)
        far_forward(it)
        for side, y in enumerate((0, cy - 1)):
            for x in range(cx):
                ysend[it, side, :, pl.ds(x * cz, cz)] = wpad[
                    :, pl.ds(((x + 1) * pad_y + y + 1) * cz, cz)
                ].astype(BF16)
            face_start(it, 1, side)

        def gather(j, carry):
            low, high = carry
            first = wpad[:, pl.ds(pl.multiple_of(padded(j), 128), 128)]
            last = wpad[:, pl.ds(pl.multiple_of(padded(j) + cz - 128, 128), 128)]
            low = jnp.where(narrow == j, pltpu.roll(first, j, 1), low)
            high = jnp.where(narrow == j, pltpu.roll(last, j + 1, 1), high)
            return low, high

        empty = jnp.zeros((rows, 128), F32)
        low, high = lax.fori_loop(0, cx * cy, gather, (empty, empty))
        zsend[it, 0] = low.astype(BF16)
        zsend[it, 1] = high.astype(BF16)
        face_start(it, 2, 0)
        face_start(it, 2, 1)

        def apply_inside(j):
            res_ref[:, cols(j)] = (
                field[:, cols(j)]
                - row(1, j) * smooth[:, cols(j)]
                + row(0, j) * beside(padded(j))
            )

        each(0, cx * cy, apply_inside)

        face_wait(it, 2, 0)
        face_wait(it, 2, 1)
        zlow, zhigh = zrecv[it, 0].astype(F32), zrecv[it, 1].astype(F32)

        def add_z(j):
            first = pl.ds(pl.multiple_of(j * cz, 128), 128)
            last = pl.ds(pl.multiple_of(j * cz + cz - 128, 128), 128)
            scale = coef[0, pl.ds(j, 1), :]
            res_ref[:, first] = res_ref[:, first] + jnp.where(
                narrow == 0, scale[:, :128] * pltpu.roll(zlow, (128 - j) % 128, 1), 0.0
            )
            res_ref[:, last] = res_ref[:, last] + jnp.where(
                narrow == 127, scale[:, cz - 128 :] * pltpu.roll(zhigh, 127 - j, 1), 0.0
            )

        each(0, cx * cy, add_z)
        for side, y in enumerate((0, cy - 1)):
            face_wait(it, 1, side)
            for x in range(cx):
                j = x * cy + y
                part = pl.ds(j * cz, cz)
                res_ref[:, part] = res_ref[:, part] + coef[0, pl.ds(j, 1), :] * yrecv[
                    it, side, :, pl.ds(x * cz, cz)
                ].astype(F32)
        for turn, side in enumerate((1 - a % 2, a % 2)):
            if turn == 1 and it < ITERS - 1:
                coarse_rhs = restrict(False)
            face_wait(it, 0, side)
            if turn == 1:
                far_wait(it)
            x = side * (cx - 1)
            terms = []
            for y in range(cy):
                j = x * cy + y
                term = row(0, j) * xrecv[it, side, :, pl.ds(y * cz, cz)].astype(F32)
                res_ref[:, cols(j)] = res_ref[:, cols(j)] + term
                terms.append(term.astype(BF16))
            if turn == 1 and it < ITERS - 1:
                coarse_rhs = coarse_rhs + restrict_layer(jnp.concatenate(terms, axis=1), x)

    for it in range(ITERS):
        far_drain(it)
        for step in range(CHEB):
            line_drain(CHEB * it + step)
        for which in range(3):
            face_drain(it, which)
    others = owners.at[pl.ds(0, n_gz - 1)]
    pltpu.make_async_copy(others, others, owner_send_sem).wait()


def emit(sol_ref, res_ref, sol_out, res_out, sem):
    rows, cx, cy, cz = sol_out.shape
    copies = []
    for which, (source, target) in enumerate(((sol_ref, sol_out), (res_ref, res_out))):
        for x in range(cx):
            for y in range(cy):
                copies.append(
                    pltpu.make_async_copy(
                        source.at[:, pl.ds((x * cy + y) * cz, cz)],
                        target.at[:, x, y, :],
                        sem.at[which, x, y],
                    )
                )
    for copy in copies:
        copy.start()
    for copy in copies:
        copy.wait()


def local(sizes, right_side, stiffness, reaction, deflation, coarse_blocks, row_owner, neighbours):
    n_gx, n_gy, n_gz = sizes
    rows, cx, cy, cz = right_side.shape
    cells = cx * cy * cz
    vectors = deflation.shape[0]
    vmem = pl.BlockSpec(memory_space=pltpu.VMEM)
    smem = pl.BlockSpec(memory_space=pltpu.SMEM)
    hbm = pl.BlockSpec(memory_space=pl.ANY)
    turns = ITERS * CHEB
    flat = jax.ShapeDtypeStruct((rows, cells), F32)
    solution, residual = pl.pallas_call(
        functools.partial(kernel, (n_gx, n_gy, n_gz, cx, cy, cz)),
        out_shape=(flat, flat),
        in_specs=[hbm] * 3 + [vmem] * 2 + [smem] * 2,
        out_specs=(vmem, vmem),
        scratch_shapes=[
            pltpu.VMEM((2, cx * cy, cz), F32),
            pltpu.VMEM((4, cx * cy, cz), F32),
            pltpu.VMEM((rows, (cx + 2) * (cy + 2) * cz), F32),
            pltpu.VMEM((rows, cells), F32),
            pltpu.VMEM((7 * vectors, vectors), BF16),
            pltpu.VMEM((n_gz, 1, 128), jnp.int32),
            *[pltpu.VMEM((n_gz, rows, vectors), BF16)] * turns,
            pltpu.VMEM((ITERS, 2, rows, cy * cz), BF16),
            pltpu.VMEM((ITERS, 2, rows, cy * cz), BF16),
            pltpu.VMEM((ITERS, 2, rows, cx * cz), BF16),
            pltpu.VMEM((ITERS, 2, rows, cx * cz), BF16),
            pltpu.VMEM((ITERS, 2, rows, 128), BF16),
            pltpu.VMEM((ITERS, 2, rows, 128), BF16),
            pltpu.SemaphoreType.DMA,
            pltpu.SemaphoreType.DMA,
            pltpu.SemaphoreType.DMA((turns, n_gz)),
            pltpu.SemaphoreType.DMA((turns, n_gz)),
            pltpu.SemaphoreType.DMA((ITERS, 3, 2)),
            pltpu.SemaphoreType.DMA((ITERS, 3, 2)),
            pltpu.SemaphoreType.DMA((cx, cy)),
            pltpu.SemaphoreType.DMA((2, cx)),
            pltpu.VMEM((ITERS, rows, max(SHARES)), BF16),
            pltpu.SemaphoreType.DMA((ITERS, 2, len(SHARES))),
            pltpu.SemaphoreType.DMA((ITERS, 2, len(SHARES))),
        ],
        compiler_params=pltpu.CompilerParams(
            collective_id=0, has_side_effects=True, vmem_limit_bytes=28 * 1024 * 1024
        ),
        name="schwarz",
    )(
        right_side,
        stiffness,
        reaction,
        deflation.reshape(vectors, cells),
        coarse_blocks.reshape(7 * vectors, vectors),
        row_owner,
        neighbours,
    )
    whole = jax.ShapeDtypeStruct(right_side.shape, F32)
    return pl.pallas_call(
        emit,
        out_shape=(whole, whole),
        in_specs=[vmem, vmem],
        out_specs=(hbm, hbm),
        scratch_shapes=[pltpu.SemaphoreType.DMA((2, cx, cy))],
        compiler_params=pltpu.CompilerParams(vmem_limit_bytes=4 * 1024 * 1024),
        name="emit",
    )(solution, residual)


def solution(mesh):
    sizes = tuple(mesh.shape[name] for name in ("gx", "gy", "gz"))
    return jax.shard_map(
        functools.partial(local, sizes),
        mesh=mesh,
        in_specs=(
            P(None, "gx", "gy", "gz"),
            P("gx", "gy", "gz"),
            P("gx", "gy", "gz"),
            P(None, "gx", "gy", "gz"),
            P(("gx", "gy", "gz"), None, None, None),
            P(("gx", "gy", "gz")),
            P(("gx", "gy", "gz"), None),
        ),
        out_specs=(P(None, "gx", "gy", "gz"), P(None, "gx", "gy", "gz")),
        check_vma=False,
    )
```
